128 devices in a mesh: grp: 32 (over y, x, core), own: 4 (over z).
Axes of the slice: x: 4, y: 4, z: 4, core: 2. Of those that a mesh axis runs over, the one named last changes fastest.
Arguments:
- background: bfloat16 [256, 1024, 512], P('grp', 'own'), may hold values from -6 to 6
- obs_ens: bfloat16 [256, 2048, 512], P('grp', 'own'), may hold values from -12 to 12
- innovation: bfloat16 [256, 2048], P('grp', 'own'), may hold values from -6 to 6
- obs_weight: bfloat16 [256, 2048], P('grp', 'own'), may hold values from 0.25 to 4
- obs_count: int32 [256, 4], P('grp', 'own'), may hold values from 128 to 512, as said below
- dest: int32 [256], replicated, may hold values from 0 to 31, as said below
Outputs:
- analysis: bfloat16 [256, 1024, 512], P('grp', 'own')
The draws below stay inside these ranges and needn't reach their ends.
Inputs may be any that keep to these rules, and one draw needn't show every extreme that they name: `obs_count`: each entry counts the live leading slots of one owner's block of 512; later slots carry values that must be ignored. The largest entry of every draw equals 512. `dest`: every index of grp is named by exactly 8 groups, and no two groups of one index of grp name the same index.
All inputs are finite; a program needn't handle non-finite values.
Results may differ from the reference program's by a relative error of at most 0.012.
The reference program's roundings to bfloat16 on the way (of `obs_pert`, `weight`, `source`, `weighted`, `inverse`, `weights`, `state_pert` and `result`) count: a program that leaves them out, or rounds other values in their place, can miss the bound.
Values may be sent and summed in bfloat16 or wider, within the bound.
A program may use at most 128 MiB of HBM per device.

```python
import math
import jax
import jax.numpy as jnp
from jax import lax

MEMBERS = 512
G_DEV = 8
OBS_OWN = 512
NS_IT = 4
ROWS = 1024
OBS = 2048
GROUPS = 256


def draw_obs_ens(key, part):
    subkeys = jax.random.split(key, 2)
    row_scale = jnp.exp(jax.random.uniform(subkeys[0], (GROUPS, OBS, 1), minval=math.log(0.3), maxval=math.log(3.0)))
    values = jax.random.normal(subkeys[1], (GROUPS, OBS, MEMBERS)) * row_scale
    return jnp.clip(values, -12.0, 12.0).astype(jnp.bfloat16)


def draw_obs_count(key, part):
    subkeys = jax.random.split(key, 4)
    host_total = GROUPS // G_DEV
    owners = OBS // OBS_OWN
    floor_count = OBS_OWN // 4
    density = jax.random.randint(subkeys[0], (host_total,), 1, 9)
    density = density.at[jax.random.randint(subkeys[1], (), 0, host_total)].set(8)
    ceiling = floor_count + density * (OBS_OWN - floor_count) // 8
    ceiling_rows = jnp.repeat(ceiling, G_DEV)[:, None]
    counts = jax.random.randint(subkeys[2], (GROUPS, owners), floor_count, ceiling_rows + 1)
    chosen = jax.random.randint(subkeys[3], (), 0, GROUPS * owners)
    flattened = counts.reshape(-1).at[chosen].set(OBS_OWN)
    return flattened.reshape(GROUPS, owners).astype(jnp.int32)


def draw_dest(key, part):
    subkeys = jax.random.split(key, 2)
    host_total = GROUPS // G_DEV
    shuffle = jax.random.permutation(subkeys[0], host_total)
    offsets = jax.random.permutation(subkeys[1], host_total)[:G_DEV]
    target = (shuffle[:, None] + offsets[None, :]) % host_total
    return target.reshape(GROUPS).astype(jnp.int32)


def block_scale(stream_key, dims, pieces, least, top_value):
    loudness = 1.0
    for dim, parts in pieces:
        draws = jax.random.uniform(jax.random.fold_in(jax.random.fold_in(stream_key, 6), dim), (parts,), jnp.float32, least / len(pieces), top_value / len(pieces))
        loudness = loudness * jnp.repeat(jnp.exp(draws), dims[dim] // parts).reshape((-1,) + (1,) * (len(dims) - 1 - dim))
    return loudness


def noise(stream_key, extent, spread, reach, shards=(), kind=jnp.bfloat16):
    gain = block_scale(stream_key, extent, shards, -0.22, 0.18) if shards else 1.0
    values = jax.random.normal(stream_key, extent, jnp.float32) * spread * gain
    return jnp.minimum(jnp.maximum(values, -reach), reach).astype(kind)


def setup_inputs(seed: int = 0) -> dict:
    seeds = jax.random.split(jax.random.key(seed), 7)
    background = noise(seeds[0], (GROUPS, ROWS, MEMBERS), 1.0, 6.0, ((0, 32), (1, 4)))
    obs_ens = draw_obs_ens(jax.random.fold_in(seeds[6], 71), 0)
    innovation = noise(seeds[2], (GROUPS, OBS), 1.0, 6.0, ((0, 32), (1, 4)))
    obs_weight = jnp.clip(jnp.exp(math.log(4.0) - 2.7725887 * jax.random.uniform(seeds[3], (GROUPS, OBS), jnp.float32) ** block_scale(seeds[3], (GROUPS, OBS), ((0, 32), (1, 4)), -0.2, 0.2)), 0.25, 4.0).astype(jnp.bfloat16)
    obs_count = draw_obs_count(jax.random.fold_in(seeds[6], 71), 0)
    dest = draw_dest(jax.random.fold_in(seeds[6], 71), 0)
    return dict(background=background, obs_ens=obs_ens, innovation=innovation, obs_weight=obs_weight, obs_count=obs_count, dest=dest)


def newton_weights(gram, right_side):
    eye_mat = jnp.eye(MEMBERS, dtype=jnp.float32)
    matrix = gram + (MEMBERS - 1.0) * eye_mat
    norm_scale = jnp.sqrt(jnp.sum(matrix * matrix))
    root_iter = (matrix / norm_scale).astype(jnp.bfloat16)
    inverse = eye_mat.astype(jnp.bfloat16)
    for iteration in range(NS_IT):
        product = jnp.dot(inverse, root_iter, preferred_element_type=jnp.float32)
        factor = (1.5 * eye_mat - 0.5 * product).astype(jnp.bfloat16)
        root_iter = jnp.dot(root_iter, factor, preferred_element_type=jnp.float32).astype(jnp.bfloat16)
        inverse = jnp.dot(factor, inverse, preferred_element_type=jnp.float32).astype(jnp.bfloat16)
    inverse_wide = inverse.astype(jnp.float32)
    half_way = jnp.dot(inverse_wide, right_side, precision=lax.Precision.HIGHEST)
    mean_weight = jnp.dot(inverse_wide, half_way, precision=lax.Precision.HIGHEST) / norm_scale
    weights = jnp.sqrt((MEMBERS - 1.0) / norm_scale) * inverse_wide + mean_weight[:, None]
    return weights.astype(jnp.bfloat16)

def analyse(items):
    background, obs_ens, innovation, obs_weight, counts = items
    obs_mean = lax.optimization_barrier(jnp.mean(obs_ens.astype(jnp.float32), axis=1, keepdims=True))
    obs_pert = (obs_ens.astype(jnp.float32) - obs_mean).astype(jnp.bfloat16)
    position_in = jnp.arange(OBS) % OBS_OWN
    live_rows = position_in < jnp.repeat(counts, OBS_OWN)
    weight = jnp.where(live_rows, obs_weight, jnp.zeros_like(obs_weight)).astype(jnp.bfloat16)
    source = (weight.astype(jnp.float32) * innovation.astype(jnp.float32)).astype(jnp.bfloat16)
    weighted = (obs_pert.astype(jnp.float32) * weight.astype(jnp.float32)[:, None]).astype(jnp.bfloat16)
    gram = jnp.dot(weighted.T, obs_pert, preferred_element_type=jnp.float32)
    right_side = jnp.dot(source, obs_pert, preferred_element_type=jnp.float32)
    weights = newton_weights(gram, right_side)
    state_mean = lax.optimization_barrier(jnp.mean(background.astype(jnp.float32), axis=1, keepdims=True))
    state_pert = (background.astype(jnp.float32) - state_mean).astype(jnp.bfloat16)
    result = state_mean + jnp.dot(state_pert, weights, preferred_element_type=jnp.float32)
    return result.astype(jnp.bfloat16)

def reference(background, obs_ens, innovation, obs_weight, obs_count, dest):
    results = lax.map(analyse, (background, obs_ens, innovation, obs_weight, obs_count))
    group_ids = jnp.arange(GROUPS).astype(jnp.int32)
    same_dest = dest[None, :] == dest[:, None]
    earlier = group_ids[None, :] < group_ids[:, None]
    arrival_rank = lax.optimization_barrier(jnp.sum(jnp.where(same_dest & earlier, 1, 0), axis=1)).astype(jnp.int32)
    slot_of = (dest * G_DEV + arrival_rank).astype(jnp.int32)
    holder = lax.optimization_barrier(jnp.sum(jnp.where(slot_of[None, :] == group_ids[:, None], group_ids[None, :], 0), axis=1)).astype(jnp.int32)
    return results[holder]
```

```python
import jax
import jax.numpy as jnp
from jax import lax
from jax.sharding import PartitionSpec as P

NS_IT = 4


def newton_weights(gram, right_side):
    members = gram.shape[-1]
    eye_mat = jnp.eye(members, dtype=jnp.float32)
    matrix = gram + (members - 1.0) * eye_mat
    norm_scale = jnp.sqrt(jnp.sum(matrix * matrix, axis=(1, 2)))
    root_iter = (matrix / norm_scale[:, None, None]).astype(jnp.bfloat16)
    inverse = jnp.broadcast_to(eye_mat.astype(jnp.bfloat16), matrix.shape)
    for iteration in range(NS_IT):
        product = jnp.einsum("gij,gjk->gik", inverse, root_iter, preferred_element_type=jnp.float32)
        factor = (1.5 * eye_mat - 0.5 * product).astype(jnp.bfloat16)
        root_iter = jnp.einsum(
            "gij,gjk->gik", root_iter, factor, preferred_element_type=jnp.float32
        ).astype(jnp.bfloat16)
        inverse = jnp.einsum(
            "gij,gjk->gik", factor, inverse, preferred_element_type=jnp.float32
        ).astype(jnp.bfloat16)
    inverse_wide = inverse.astype(jnp.float32)
    half_way = jnp.einsum("gij,gj->gi", inverse_wide, right_side)
    mean_weight = jnp.einsum("gij,gj->gi", inverse_wide, half_way) / norm_scale[:, None]
    weights = (
        jnp.sqrt((members - 1.0) / norm_scale)[:, None, None] * inverse_wide
        + mean_weight[:, :, None]
    )
    return weights.astype(jnp.bfloat16)


def solve_weights(obs_pert, weight, source):
    weighted = (obs_pert.astype(jnp.float32) * weight.astype(jnp.float32)[:, :, None]).astype(
        jnp.bfloat16
    )
    gram_local = jnp.einsum("gpk,gpl->gkl", weighted, obs_pert, preferred_element_type=jnp.float32)
    right_local = jnp.einsum("gp,gpk->gk", source, obs_pert, preferred_element_type=jnp.float32)
    gram_part, right_part = (
        lax.psum_scatter(gram_local, "own", scatter_dimension=0, tiled=True),
        lax.psum_scatter(right_local, "own", scatter_dimension=0, tiled=True),
    )
    return lax.all_gather(newton_weights(gram_part, right_part), "own", axis=0, tiled=True)


def apply_weights(state_here, weights):
    state_mean = jnp.mean(state_here.astype(jnp.float32), axis=2, keepdims=True)
    state_pert = (state_here.astype(jnp.float32) - state_mean).astype(jnp.bfloat16)
    result = state_mean + jnp.einsum(
        "grk,gkl->grl", state_pert, weights, preferred_element_type=jnp.float32
    )
    return result.astype(jnp.bfloat16)


def route(result, dest):
    grp_size = lax.axis_size("grp")
    local_groups, rows, members = result.shape
    group_total = dest.shape[0]
    group_ids = jnp.arange(group_total, dtype=jnp.int32)
    same_dest = dest[None, :] == dest[:, None]
    earlier = group_ids[None, :] < group_ids[:, None]
    arrival_rank = jnp.sum(jnp.where(same_dest & earlier, 1, 0), axis=1).astype(jnp.int32)
    slot_of = dest * local_groups + arrival_rank
    holder = jnp.sum(
        jnp.where(slot_of[None, :] == group_ids[:, None], group_ids[None, :], 0), axis=1
    ).astype(jnp.int32)
    piece = rows // grp_size
    pieces = result.reshape(local_groups, grp_size, piece, members).swapaxes(0, 1)
    spread = lax.all_to_all(pieces, "grp", split_axis=0, concat_axis=0, tiled=True)
    spread = spread.reshape(group_total, piece, members)
    ordered = jnp.take(spread, holder, axis=0).reshape(grp_size, local_groups, piece, members)
    back = lax.all_to_all(ordered, "grp", split_axis=0, concat_axis=0, tiled=True)
    return back.swapaxes(0, 1).reshape(local_groups, rows, members)


def body(background, obs_ens, innovation, obs_weight, obs_count, dest):
    local_groups = background.shape[0]
    obs_rows = obs_ens.shape[1]
    obs_mean = jnp.mean(obs_ens.astype(jnp.float32), axis=2, keepdims=True)
    obs_pert = (obs_ens.astype(jnp.float32) - obs_mean).astype(jnp.bfloat16)
    position_in = lax.broadcasted_iota(jnp.int32, (local_groups, obs_rows), 1)
    live_rows = position_in < obs_count
    weight = jnp.where(live_rows, obs_weight, jnp.zeros_like(obs_weight))
    source = (weight.astype(jnp.float32) * innovation.astype(jnp.float32)).astype(jnp.bfloat16)
    weights = solve_weights(obs_pert, weight, source)
    result = apply_weights(background, weights)
    return route(result, dest)


def solution(mesh):
    return jax.shard_map(
        body,
        mesh=mesh,
        in_specs=(
            P("grp", "own", None),
            P("grp", "own", None),
            P("grp", "own"),
            P("grp", "own"),
            P("grp", "own"),
            P(),
        ),
        out_specs=P("grp", "own", None),
        check_vma=False,
    )
```

```python
import random

import jax
import jax.numpy as jnp
from jax import lax
from jax.experimental import pallas as pl
from jax.experimental.pallas import tpu as pltpu
from jax.sharding import PartitionSpec as P

MESH = pl.DeviceIdType.MESH
F32 = jnp.float32
BF16 = jnp.bfloat16
MEMBERS = 512
HALF = 256
GROUPS_HERE = 8
ROUNDS = 2
GRP = 32

ORDER = list(range(1, GRP))
random.Random(23).shuffle(ORDER)


def dot(a, b):
    return jnp.dot(a, b, preferred_element_type=F32)


def dot_nt(a, b):
    return lax.dot_general(a, b, (((1,), (1,)), ((), ())), preferred_element_type=F32)


def eye(n):
    rows = lax.broadcasted_iota(jnp.int32, (n, n), 0)
    cols = lax.broadcasted_iota(jnp.int32, (n, n), 1)
    return jnp.where(rows == cols, 1.0, 0.0).astype(F32)


def kernel(
    holder, obs_hbm, bg_hbm, innov, obs_weight, count, out,
    obs, bg, wrow, src, part, own_part, relay_own, relay_in, owner_in, rhs_part, rhs_in,
    root, inv, fac, vbuf, mwbuf, pert, mean, spread, gathered, picked,
    obs_sem, bg_sem, send_z, recv_z, send_g, recv_g, self_sem,
):
    me = lax.axis_index("grp")
    z = lax.axis_index("own")
    y, x, c = me // 8, lax.rem(me // 2, 4), lax.rem(me, 2)

    def peer(s):
        return (
            lax.rem(y + s // 8, 4) * 8 + lax.rem(x + (s // 2) % 4, 4) * 2 + lax.rem(c + s % 2, 2)
        )

    def zpeer(q):
        return lax.rem(z + q, 4)

    def group(r, q):
        return zpeer(q) * ROUNDS + r

    barrier = pltpu.get_barrier_semaphore()
    for s in ORDER:
        pl.semaphore_signal(barrier, inc=1, device_id={"grp": peer(s)}, device_id_type=MESH)
    for q in (1, 2, 3):
        pl.semaphore_signal(barrier, inc=1, device_id={"own": zpeer(q)}, device_id_type=MESH)

    loads = []
    for r in range(ROUNDS):
        for q in (2, 1, 3, 0):
            load = pltpu.make_async_copy(
                obs_hbm.at[group(r, q)], obs.at[group(r, q)], obs_sem.at[r, q]
            )
            load.start()
            loads.append(load)
    bg_load = pltpu.make_async_copy(bg_hbm, bg, bg_sem)
    bg_load.start()

    position = lax.broadcasted_iota(jnp.int32, (GROUPS_HERE, 512), 1)
    weight = jnp.where(position < count[...], obs_weight[...].astype(F32), 0.0)
    source = (weight * innov[...].astype(F32)).astype(BF16)
    for g in range(GROUPS_HERE):
        wrow[g] = jnp.broadcast_to(weight[g : g + 1], (8, 512))
        src[g] = jnp.broadcast_to(source[g : g + 1].astype(F32), (16, 512)).astype(BF16)

    pending = []

    def zcopy(source_ref, target_ref, q, r, index):
        copy = pltpu.make_async_remote_copy(
            src_ref=source_ref,
            dst_ref=target_ref,
            send_sem=send_z.at[r, index],
            recv_sem=recv_z.at[r, index],
            device_id={"own": zpeer(q)},
            device_id_type=MESH,
        )
        copy.start()
        pending.append(copy)
        return copy

    def gram(r, q):
        g = group(r, q)
        ens = obs[g].astype(F32)
        centred = (ens - jnp.mean(ens, axis=1, keepdims=True)).astype(BF16)
        turned = (centred.astype(F32).T * wrow[g][0:1]).astype(BF16)
        upper = dot(turned[:HALF], centred)
        corner = dot(turned[HALF:], centred[:, HALF:])
        right = dot(src[g], centred)[0:8]
        return (upper[:, :HALF], upper[:, HALF:], corner), right

    relay = {}
    direct = {}
    for r in range(ROUNDS):
        for n, q in enumerate((2, 1, 3, 0)):
            loads[r * 4 + n].wait()
            blocks, right = gram(r, q)
            if r == 0 and n == 0:
                pl.semaphore_wait(barrier, GRP - 1 + 3)
            if q == 0:
                for b in range(3):
                    own_part[r, b] = blocks[b]
                rhs_part[r, 0] = right
                continue
            for b in range(3):
                for h in range(2):
                    piece = blocks[b][h * 128 : (h + 1) * 128]
                    if (q, h) in ((1, 0), (3, 1)):
                        relay_own[r, h, b] = piece
                    else:
                        part[r, q, h, b] = piece.astype(BF16)
            rhs_part[r, q] = right
            if q == 2:
                relay[r, 0] = zcopy(part.at[r, 2, 0], relay_in.at[r, 0], 1, r, 0)
                relay[r, 1] = zcopy(part.at[r, 2, 1], relay_in.at[r, 1], 3, r, 1)
            elif q == 1:
                direct[r, 1] = zcopy(part.at[r, 1, 1], owner_in.at[r, 0, 1], 1, r, 2)
            else:
                direct[r, 0] = zcopy(part.at[r, 3, 0], owner_in.at[r, 1, 0], 3, r, 3)
            direct[r, 1 + q] = zcopy(rhs_part.at[r, q], rhs_in.at[r, q], q, r, 3 + q)
        if r == 0:
            continue
    combined = {}
    for r in range(ROUNDS):
        for h, q in ((0, 1), (1, 3)):
            relay[r, h].wait_recv()
            for b in range(3):
                part[r, q, h, b] = (relay_own[r, h, b] + relay_in[r, h, b].astype(F32)).astype(BF16)
            combined[r, h] = zcopy(
                part.at[r, q, h], owner_in.at[r, 0 if q == 1 else 1, h], q, r, 7 + h
            )

    bg_load.wait()
    for g in range(GROUPS_HERE):
        state = bg[g].astype(F32)
        centre = jnp.mean(state, axis=1, keepdims=True)
        pert[g] = (state - centre).astype(BF16)
        mean[g] = jnp.broadcast_to(centre, (256, 128))

    def sym_rows(rows, blocks):
        high = rows.astype(BF16)
        low = (rows - high.astype(F32)).astype(BF16)
        both = jnp.concatenate([high, low], axis=0)
        a, b = both[:, :HALF], both[:, HALF:]
        left = dot(a, blocks[0]) + dot_nt(b, blocks[1])
        right = dot(a, blocks[1]) + dot(b, blocks[2])
        full = jnp.concatenate([left, right], axis=1)
        return full[0:16] + full[16:32]

    gathers = {}
    for r in range(ROUNDS):
        for h in range(2):
            direct[r, h].wait_recv()
            combined[r, h].wait_recv()
        for q in (1, 2, 3):
            direct[r, 1 + q].wait_recv()
        blocks = []
        for b in range(3):
            total = own_part[r, b]
            total = total + owner_in[r, 0, :, b].astype(F32).reshape(HALF, HALF)
            total = total + owner_in[r, 1, :, b].astype(F32).reshape(HALF, HALF)
            if b != 1:
                total = total + (MEMBERS - 1.0) * eye(HALF)
            blocks.append(total)
        squares = (
            jnp.sum(blocks[0] * blocks[0])
            + 2.0 * jnp.sum(blocks[1] * blocks[1])
            + jnp.sum(blocks[2] * blocks[2])
        )
        scale = jnp.sqrt(jnp.full((1, 1), squares, F32))
        per = 1.0 / scale
        cross = blocks[1] * per
        root[:HALF, :HALF] = (blocks[0] * per).astype(BF16)
        root[:HALF, HALF:] = cross.astype(BF16)
        root[HALF:, :HALF] = cross.T.astype(BF16)
        root[HALF:, HALF:] = (blocks[2] * per).astype(BF16)
        unit = eye(MEMBERS)
        fac[...] = (1.5 * unit - 0.5 * root[...].astype(F32)).astype(BF16)
        inv[...] = fac[...]
        root[...] = dot(root[...], fac[...]).astype(BF16)
        for _ in range(2):
            fac[...] = (1.5 * eye(MEMBERS) - 0.5 * dot(inv[...], root[...])).astype(BF16)
            root[...] = dot(root[...], fac[...]).astype(BF16)
            inv[...] = dot(fac[...], inv[...]).astype(BF16)
        fac[...] = (1.5 * eye(MEMBERS) - 0.5 * dot(inv[...], root[...])).astype(BF16)
        upper = dot(fac[:HALF], inv[...]).astype(BF16)
        corner = dot(fac[HALF:], inv[:, HALF:]).astype(BF16)
        blocks = (upper[:, :HALF], upper[:, HALF:], corner)
        right = rhs_part[r, 0] + rhs_in[r, 1] + rhs_in[r, 2] + rhs_in[r, 3]
        right = jnp.concatenate([right, right], axis=0)
        half_way = sym_rows(right, blocks)
        mwbuf[r, 0] = (sym_rows(half_way, blocks) * per)[0:8]
        gain = jnp.sqrt((MEMBERS - 1.0) * per)
        for b in range(3):
            scaled = (blocks[b].astype(F32) * gain).astype(BF16)
            for h in range(2):
                vbuf[r, 0, h, b] = scaled[h * 128 : (h + 1) * 128]
        gathers[r, 3] = zcopy(vbuf.at[r, 0], vbuf.at[r, 3], 1, r, 9)
        gathers[r, 1] = zcopy(vbuf.at[r, 0], vbuf.at[r, 1], 3, r, 10)
        for q in (1, 2, 3):
            gathers[r, 3 + q] = zcopy(mwbuf.at[r, 0], mwbuf.at[r, 4 - q], q, r, 10 + q)

    forward = {}
    for r in range(ROUNDS):
        gathers[r, 3].wait_recv()
        forward[r, 0] = zcopy(vbuf.at[r, 3, 0], vbuf.at[r, 2, 0], 1, r, 14)
        gathers[r, 1].wait_recv()
        forward[r, 1] = zcopy(vbuf.at[r, 1, 1], vbuf.at[r, 2, 1], 3, r, 15)

    def gcopy(phase, s, source_ref, target_ref):
        return pltpu.make_async_remote_copy(
            src_ref=source_ref,
            dst_ref=target_ref,
            send_sem=send_g.at[phase, s],
            recv_sem=recv_g.at[phase, s],
            device_id={"grp": peer(s)},
            device_id_type=MESH,
        )

    locals_ = []
    routed = []
    for r in range(ROUNDS):
        for q in (0, 1, 3, 2):
            if q == 1:
                for p in (1, 2, 3):
                    gathers[r, 3 + p].wait_recv()
            if q == 2:
                forward[r, 0].wait_recv()
                forward[r, 1].wait_recv()
            g = group(r, q)
            left, right = pert[g, :, :HALF], pert[g, :, HALF:]
            v = [vbuf[r, q, :, b].reshape(HALF, HALF) for b in range(3)]
            shift = jnp.sum(pert[g].astype(F32) * mwbuf[r, q][0:1], axis=1, keepdims=True)
            shift = shift + mean[g][:, 0:1]
            cols = (
                dot(left, v[0]) + dot_nt(right, v[1]) + shift,
                dot(left, v[1]) + dot(right, v[2]) + shift,
            )
            for h in range(2):
                block = cols[h].astype(BF16)
                for b in range(16):
                    spread[r, h * 16 + b, zpeer(q)] = block[b * 16 : (b + 1) * 16]
        for s in ORDER:
            copy = gcopy(r, s, spread.at[r, peer(s)], gathered.at[pl.ds(r * 128 + me * 4, 4)])
            copy.start()
            routed.append(copy)
        mine = pltpu.make_async_copy(
            spread.at[r, me], gathered.at[pl.ds(r * 128 + me * 4, 4)], self_sem.at[r]
        )
        mine.start()
        locals_.append(mine)
    for copy in routed:
        copy.wait_recv()
    for copy in locals_:
        copy.wait()

    row = pl.multiple_of(lax.rem(me, 16) * 16, 16)
    col = pl.multiple_of((me // 16) * HALF, HALF)
    final = []

    def pick(s):
        d = peer(s)
        for k in range(GROUPS_HERE):
            picked[d, k] = gathered[holder[d * GROUPS_HERE + k]]

    def send(s):
        target = out.at[:, pl.ds(row, 16), pl.ds(col, HALF)]
        if s == 0:
            copy = pltpu.make_async_copy(picked.at[me], target, self_sem.at[2])
        else:
            copy = gcopy(2, s, picked.at[peer(s)], target)
        copy.start()
        final.append(copy)

    order = ORDER + [0]
    pick(order[0])
    for n in range(GRP):
        if n + 1 < GRP:
            pick(order[n + 1])
        send(order[n])
    for copy in pending + routed:
        copy.wait_send()
    for copy in final:
        copy.wait()


def analyse(background, obs_ens, innovation, obs_weight, obs_count, holder):
    vmem = pltpu.VMEM
    any_spec = pl.BlockSpec(memory_space=pl.ANY)
    vmem_spec = pl.BlockSpec(memory_space=pltpu.VMEM)
    return pl.pallas_call(
        kernel,
        out_shape=jax.ShapeDtypeStruct(background.shape, BF16),
        in_specs=[
            pl.BlockSpec(memory_space=pltpu.SMEM), any_spec, any_spec,
            vmem_spec, vmem_spec, vmem_spec,
        ],
        out_specs=any_spec,
        scratch_shapes=[
            vmem((8, 512, 512), BF16),
            vmem((8, 256, 512), BF16),
            vmem((8, 8, 512), F32),
            vmem((8, 16, 512), BF16),
            vmem((2, 4, 2, 3, 128, 256), BF16),
            vmem((2, 3, 256, 256), F32),
            vmem((2, 2, 3, 128, 256), F32),
            vmem((2, 2, 3, 128, 256), BF16),
            vmem((2, 2, 2, 3, 128, 256), BF16),
            vmem((2, 4, 8, 512), F32),
            vmem((2, 4, 8, 512), F32),
            vmem((512, 512), BF16),
            vmem((512, 512), BF16),
            vmem((512, 512), BF16),
            vmem((2, 4, 2, 3, 128, 256), BF16),
            vmem((2, 4, 8, 512), F32),
            vmem((8, 256, 512), BF16),
            vmem((8, 256, 128), F32),
            vmem((2, 32, 4, 16, 256), BF16),
            vmem((256, 16, 256), BF16),
            vmem((32, 8, 16, 256), BF16),
            pltpu.SemaphoreType.DMA((2, 4)),
            pltpu.SemaphoreType.DMA,
            pltpu.SemaphoreType.DMA((2, 16)),
            pltpu.SemaphoreType.DMA((2, 16)),
            pltpu.SemaphoreType.DMA((3, 32)),
            pltpu.SemaphoreType.DMA((3, 32)),
            pltpu.SemaphoreType.DMA((3,)),
        ],
        compiler_params=pltpu.CompilerParams(
            collective_id=0, has_side_effects=True, vmem_limit_bytes=60 * 1024 * 1024
        ),
    )(holder, obs_ens, background, innovation, obs_weight, obs_count)


def holder_index(dest, local_groups):
    group_total = dest.shape[0]
    group_ids = jnp.arange(group_total, dtype=jnp.int32)
    same_dest = dest[None, :] == dest[:, None]
    earlier = group_ids[None, :] < group_ids[:, None]
    arrival_rank = jnp.sum(jnp.where(same_dest & earlier, 1, 0), axis=1).astype(jnp.int32)
    slot_of = dest * local_groups + arrival_rank
    local = group_ids % local_groups
    place = (local % ROUNDS) * 128 + (group_ids // local_groups) * 4 + local // ROUNDS
    return jnp.sum(
        jnp.where(slot_of[None, :] == group_ids[:, None], place[None, :], 0), axis=1
    ).astype(jnp.int32)


def body(background, obs_ens, innovation, obs_weight, obs_count, dest):
    holder = holder_index(dest, background.shape[0])
    return analyse(background, obs_ens, innovation, obs_weight, obs_count, holder)


def solution(mesh):
    return jax.shard_map(
        body,
        mesh=mesh,
        in_specs=(
            P("grp", "own", None),
            P("grp", "own", None),
            P("grp", "own"),
            P("grp", "own"),
            P("grp", "own"),
            P(),
        ),
        out_specs=P("grp", "own", None),
        check_vma=False,
    )
```

```python
import jax
import jax.numpy as jnp
from jax import lax
from jax.experimental import pallas as pl
from jax.experimental.pallas import tpu as pltpu
from jax.sharding import PartitionSpec as P

MESH = pl.DeviceIdType.MESH
F32 = jnp.float32
BF16 = jnp.bfloat16
MEMBERS = 512
B = 128
GROUPS_HERE = 8
ROUNDS = 2
GRP = 32
STRIDE = 12
BLOCKS = [(i, j) for i in range(4) for j in range(i, 4)]


def dot(a, b):
    return jnp.dot(a, b, preferred_element_type=F32)


def dot_nt(a, b):
    return lax.dot_general(a, b, (((1,), (1,)), ((), ())), preferred_element_type=F32)


def eye(n):
    rows = lax.broadcasted_iota(jnp.int32, (n, n), 0)
    cols = lax.broadcasted_iota(jnp.int32, (n, n), 1)
    return jnp.where(rows == cols, 1.0, 0.0).astype(F32)


def span(i):
    return slice(i * B, (i + 1) * B)


def kernel(
    dest_hbm, obs_hbm, bg_hbm, innov_hbm, weight_hbm, count_hbm, out,
    dest, innov, obs_weight, count,
    obs, bg, wrow, src, part, own_part, relay_own, relay_in, owner_in, rhs_part, rhs_in,
    root, inv, fac, full, vbuf, mwbuf, pert, mean, spread, gathered, picked, holder_v, holder,
    obs_sem, bg_sem, send_z, recv_z, send_g, recv_g, self_sem, small_sem,
):
    me = lax.axis_index("grp")
    z = lax.axis_index("own")
    y, x, c = me // 8, lax.rem(me // 2, 4), lax.rem(me, 2)

    def peer(s):
        return (
            lax.rem(y + s // 8, 4) * 8
            + lax.rem(x + lax.rem(s // 2, 4), 4) * 2
            + lax.rem(c + lax.rem(s, 2), 2)
        )

    def step(i):
        return 1 + lax.rem(i * STRIDE, GRP - 1)

    def zpeer(q):
        return lax.rem(z + q, 4)

    def group(r, q):
        return zpeer(q) * ROUNDS + r

    barrier = pltpu.get_barrier_semaphore()

    def greet(s, carry):
        pl.semaphore_signal(barrier, inc=1, device_id={"grp": peer(s)}, device_id_type=MESH)
        return carry

    for q in (2, 1, 3):
        pl.semaphore_signal(barrier, inc=1, device_id={"own": zpeer(q)}, device_id_type=MESH)
    lax.fori_loop(1, GRP, greet, 0)

    small = (
        (count_hbm, count), (weight_hbm, obs_weight), (innov_hbm, innov), (dest_hbm, dest)
    )
    small = [
        pltpu.make_async_copy(pair[0], pair[1], small_sem.at[n]) for n, pair in enumerate(small)
    ]
    for load in small:
        load.start()
    loads = {}
    for r in range(ROUNDS):
        for q in (2, 1, 3, 0):
            loads[r, q] = pltpu.make_async_copy(
                obs_hbm.at[group(r, q)], obs.at[group(r, q)], obs_sem.at[r, q]
            )
            loads[r, q].start()
    bg_load = pltpu.make_async_copy(bg_hbm, bg, bg_sem)
    bg_load.start()

    for load in small:
        load.wait()
    position = lax.broadcasted_iota(jnp.int32, (1, 512), 1)
    for g in range(GROUPS_HERE):
        live = position < count[:, g : g + 1]
        weight = jnp.where(live, obs_weight[g : g + 1].astype(F32), 0.0)
        source = (weight * innov[g : g + 1].astype(F32)).astype(BF16).astype(F32)
        wrow[g] = jnp.broadcast_to(weight, (8, 512))
        src[g] = jnp.broadcast_to(source, (16, 512)).astype(BF16)

    pending = []

    def zcopy(source_ref, target_ref, q, r, index):
        copy = pltpu.make_async_remote_copy(
            src_ref=source_ref,
            dst_ref=target_ref,
            send_sem=send_z.at[r, index],
            recv_sem=recv_z.at[r, index],
            device_id={"own": zpeer(q)},
            device_id_type=MESH,
        )
        copy.start()
        pending.append(copy)
        return copy

    def gram(r, q):
        loads[r, q].wait()
        g = group(r, q)
        ens = obs[g].astype(F32)
        centred = (ens - jnp.mean(ens, axis=1, keepdims=True)).astype(BF16)
        turned = (centred.astype(F32).T * wrow[g][0:1]).astype(BF16)
        rhs_part[r, q] = dot(src[g], centred)[0:8]
        for i in range(4):
            strip = dot(turned[span(i)], centred[:, i * B :])
            for j in range(i, 4):
                b = BLOCKS.index((i, j))
                h, k = b // 5, b % 5
                block = strip[:, (j - i) * B : (j - i + 1) * B]
                if q == 0:
                    own_part[r, b] = block
                elif (q, h) in ((1, 0), (3, 1)):
                    relay_own[r, h, k] = block
                else:
                    part[r, q, h, k] = block.astype(BF16)

    relay = {}
    direct = {}

    def send_parts(r, q):
        if q == 2:
            relay[r, 0] = zcopy(part.at[r, 2, 0], relay_in.at[r, 0], 1, r, 0)
            relay[r, 1] = zcopy(part.at[r, 2, 1], relay_in.at[r, 1], 3, r, 1)
        elif q == 1:
            direct[r, 1] = zcopy(part.at[r, 1, 1], owner_in.at[r, 0, 1], 1, r, 2)
        else:
            direct[r, 0] = zcopy(part.at[r, 3, 0], owner_in.at[r, 1, 0], 3, r, 3)
        direct[r, 1 + q] = zcopy(rhs_part.at[r, q], rhs_in.at[r, q], q, r, 3 + q)

    combined = {}

    def combine(r):
        for h, q in ((0, 1), (1, 3)):
            relay[r, h].wait_recv()
            part[r, q, h] = (relay_own[r, h] + relay_in[r, h].astype(F32)).astype(BF16)
            combined[r, h] = zcopy(
                part.at[r, q, h], owner_in.at[r, 0 if q == 1 else 1, h], q, r, 7 + h
            )

    gathers = {}
    forward = {}

    def newton(r):
        for h in range(2):
            direct[r, h].wait_recv()
            combined[r, h].wait_recv()
        for q in (1, 2, 3):
            direct[r, 1 + q].wait_recv()
        squares = jnp.zeros((B, B), F32)
        totals = []
        for b, (i, j) in enumerate(BLOCKS):
            h, k = b // 5, b % 5
            total = own_part[r, b] + owner_in[r, 0, h, k].astype(F32)
            total = total + owner_in[r, 1, h, k].astype(F32)
            if i == j:
                total = total + (MEMBERS - 1.0) * eye(B)
                squares = squares + total * total
            else:
                squares = squares + 2.0 * (total * total)
            own_part[r, b] = total
        scale = jnp.sqrt(jnp.full((1, 1), jnp.sum(squares), F32))
        per = 1.0 / scale
        for b, (i, j) in enumerate(BLOCKS):
            block = own_part[r, b] * per
            root[span(i), span(j)] = block.astype(BF16)
            if i != j:
                root[span(j), span(i)] = block.T.astype(BF16)
        fac[...] = (1.5 * eye(MEMBERS) - 0.5 * root[...].astype(F32)).astype(BF16)
        inv[...] = fac[...]
        root[...] = dot(root[...], fac[...]).astype(BF16)
        for _ in range(2):
            fac[...] = (1.5 * eye(MEMBERS) - 0.5 * dot(inv[...], root[...])).astype(BF16)
            root[...] = dot(root[...], fac[...]).astype(BF16)
            inv[...] = dot(fac[...], inv[...]).astype(BF16)
        fac[...] = (1.5 * eye(MEMBERS) - 0.5 * dot(inv[...], root[...])).astype(BF16)
        inv[...] = dot(fac[...], inv[...]).astype(BF16)

        def through(rows):
            high = rows.astype(BF16)
            low = (rows - high.astype(F32)).astype(BF16)
            both = dot_nt(jnp.concatenate([high, low], axis=0), inv[...])
            return both[0:16] + both[16:32]

        right = rhs_part[r, 0] + rhs_in[r, 1] + rhs_in[r, 2] + rhs_in[r, 3]
        right = jnp.concatenate([right, right], axis=0)
        mwbuf[r, 0] = (through(through(right)) * per)[0:8]
        gain = jnp.sqrt((MEMBERS - 1.0) * per)
        for b, (i, j) in enumerate(BLOCKS):
            vbuf[r, 0, b // 5, b % 5] = (inv[span(i), span(j)].astype(F32) * gain).astype(BF16)

    def gather(r):
        gathers[r, 3] = zcopy(vbuf.at[r, 0], vbuf.at[r, 3], 1, r, 9)
        gathers[r, 1] = zcopy(vbuf.at[r, 0], vbuf.at[r, 1], 3, r, 10)
        for q in (1, 2, 3):
            gathers[r, 3 + q] = zcopy(mwbuf.at[r, 0], mwbuf.at[r, 4 - q], q, r, 10 + q)

    def pass_on(r):
        gathers[r, 3].wait_recv()
        forward[r, 0] = zcopy(vbuf.at[r, 3, 0], vbuf.at[r, 2, 0], 1, r, 14)
        gathers[r, 1].wait_recv()
        forward[r, 1] = zcopy(vbuf.at[r, 1, 1], vbuf.at[r, 2, 1], 3, r, 15)
        for q in (1, 2, 3):
            gathers[r, 3 + q].wait_recv()

    def perturb():
        bg_load.wait()

        def one(g, carry):
            state = bg[g].astype(F32)
            centre = jnp.mean(state, axis=1, keepdims=True)
            pert[g] = (state - centre).astype(BF16)
            mean[g] = jnp.broadcast_to(centre, (256, B))
            return carry

        lax.fori_loop(0, GROUPS_HERE, one, 0)

    def index():
        total = GROUPS_HERE * GRP
        across = jnp.broadcast_to(dest[...], (total, total))
        down = across.T
        rows = lax.broadcasted_iota(jnp.int32, (total, total), 0)
        cols = lax.broadcasted_iota(jnp.int32, (total, total), 1)
        match = jnp.where((across == down) & (cols < rows), 1, 0)
        slot = down * GROUPS_HERE + jnp.sum(match, axis=1, keepdims=True)
        local = lax.rem(rows, GROUPS_HERE)
        owner = lax.rem(local // ROUNDS + 4 - z, 4)
        place = (lax.rem(local, ROUNDS) * 4 + owner) * GRP + rows // GROUPS_HERE
        chosen = jnp.where(slot == cols, place, 0)
        holder_v[...] = jnp.broadcast_to(jnp.sum(chosen, axis=0, keepdims=True), (8, total))
        copy = pltpu.make_async_copy(holder_v, holder, small_sem.at[4])
        copy.start()
        copy.wait()

    def gcopy(phase, s, source_ref, target_ref):
        return pltpu.make_async_remote_copy(
            src_ref=source_ref,
            dst_ref=target_ref,
            send_sem=send_g.at[phase, s],
            recv_sem=recv_g.at[phase, s],
            device_id={"grp": peer(s)},
            device_id_type=MESH,
        )

    def spread_copy(e, s):
        return gcopy(e, s, spread.at[e, peer(s)], gathered.at[e * GRP + me])

    def apply(r, q):
        g = group(r, q)
        e = r * 4 + q
        for b, (i, j) in enumerate(BLOCKS):
            block = vbuf[r, q, b // 5, b % 5]
            full[span(i), span(j)] = block
            if i != j:
                full[span(j), span(i)] = block.T
        shift = jnp.sum(pert[g].astype(F32) * mwbuf[r, q][0:1], axis=1, keepdims=True)
        shift = shift + mean[g][:, 0:1]
        for h in range(2):
            block = (dot(pert[g], full[:, h * 256 : (h + 1) * 256]) + shift).astype(BF16)
            for k in range(16):
                spread[e, h * 16 + k] = block[k * 16 : (k + 1) * 16]

        def launch(i, carry):
            spread_copy(e, step(i)).start()
            return carry

        lax.fori_loop(0, GRP - 1, launch, 0)
        mine = pltpu.make_async_copy(
            spread.at[e, me], gathered.at[e * GRP + me], self_sem.at[e]
        )
        mine.start()
        locals_.append(mine)

    locals_ = []
    for q in (2, 1, 3):
        gram(0, q)
        if q == 2:
            pl.semaphore_wait(barrier, GRP - 1 + 3)
        send_parts(0, q)
    gram(0, 0)
    for q in (2, 1, 3, 0):
        gram(1, q)
    combine(0)
    for q in (2, 1, 3):
        send_parts(1, q)
    perturb()
    index()
    newton(0)
    combine(1)
    gather(0)
    apply(0, 0)
    newton(1)
    gather(1)
    apply(1, 0)
    pass_on(0)
    apply(0, 1)
    apply(0, 3)
    pass_on(1)
    apply(1, 1)
    apply(1, 3)
    for r in range(ROUNDS):
        forward[r, 0].wait_recv()
        forward[r, 1].wait_recv()
        apply(r, 2)

    def landed(e, carry):
        def one(s, inner):
            spread_copy(e, s).wait_recv()
            return inner

        return lax.fori_loop(1, GRP, one, carry)

    lax.fori_loop(0, GROUPS_HERE, landed, 0)
    for copy in locals_:
        copy.wait()

    row = pl.multiple_of(lax.rem(me, 16) * 16, 16)
    col = pl.multiple_of((me // 16) * 256, 256)
    target = out.at[:, pl.ds(row, 16), pl.ds(col, 256)]

    def pick(d):
        for k in range(GROUPS_HERE):
            at = lax.clamp(0, holder[0, d * GROUPS_HERE + k], GROUPS_HERE * GRP - 1)
            picked[d, k] = gathered[at]

    def route(s):
        return gcopy(GROUPS_HERE, s, picked.at[peer(s)], target)

    pick(peer(step(0)))

    def move(i, carry):
        pick(peer(step(i + 1)))
        route(step(i)).start()
        return carry

    lax.fori_loop(0, GRP - 2, move, 0)
    pick(me)
    route(step(GRP - 2)).start()
    last = pltpu.make_async_copy(picked.at[me], target, self_sem.at[GROUPS_HERE])
    last.start()
    for copy in pending:
        copy.wait_send()

    def sent(e, carry):
        def one(s, inner):
            spread_copy(e, s).wait_send()
            return inner

        return lax.fori_loop(1, GRP, one, carry)

    lax.fori_loop(0, GROUPS_HERE, sent, 0)

    def done(s, carry):
        route(s).wait()
        return carry

    lax.fori_loop(1, GRP, done, 0)
    last.wait()


def analyse(background, obs_ens, innovation, obs_weight, obs_count, dest):
    vmem = pltpu.VMEM
    hbm_spec = pl.BlockSpec(memory_space=pltpu.HBM)
    return pl.pallas_call(
        kernel,
        out_shape=jax.ShapeDtypeStruct(background.shape, BF16),
        in_specs=[hbm_spec] * 6,
        out_specs=pl.BlockSpec(memory_space=pl.ANY),
        scratch_shapes=[
            vmem(dest.shape, jnp.int32),
            vmem(innovation.shape, BF16),
            vmem(obs_weight.shape, BF16),
            vmem(obs_count.shape, jnp.int32),
            vmem((8, 512, 512), BF16),
            vmem((8, 256, 512), BF16),
            vmem((8, 8, 512), F32),
            vmem((8, 16, 512), BF16),
            vmem((2, 4, 2, 5, B, B), BF16),
            vmem((2, 10, B, B), F32),
            vmem((2, 2, 5, B, B), F32),
            vmem((2, 2, 5, B, B), BF16),
            vmem((2, 2, 2, 5, B, B), BF16),
            vmem((2, 4, 8, 512), F32),
            vmem((2, 4, 8, 512), F32),
            vmem((512, 512), BF16),
            vmem((512, 512), BF16),
            vmem((512, 512), BF16),
            vmem((512, 512), BF16),
            vmem((2, 4, 2, 5, B, B), BF16),
            vmem((2, 4, 8, 512), F32),
            vmem((8, 256, 512), BF16),
            vmem((8, 256, B), F32),
            vmem((8, 32, 16, 256), BF16),
            vmem((256, 16, 256), BF16),
            vmem((32, 8, 16, 256), BF16),
            vmem((8, 256), jnp.int32),
            pltpu.SMEM((8, 256), jnp.int32),
            pltpu.SemaphoreType.DMA((2, 4)),
            pltpu.SemaphoreType.DMA,
            pltpu.SemaphoreType.DMA((2, 16)),
            pltpu.SemaphoreType.DMA((2, 16)),
            pltpu.SemaphoreType.DMA((9, 32)),
            pltpu.SemaphoreType.DMA((9, 32)),
            pltpu.SemaphoreType.DMA((9,)),
            pltpu.SemaphoreType.DMA((5,)),
        ],
        compiler_params=pltpu.CompilerParams(
            collective_id=0, has_side_effects=True, vmem_limit_bytes=44 * 1024 * 1024
        ),
    )(*(
        pltpu.with_memory_space_constraint(a, pltpu.HBM)
        for a in (dest, obs_ens, background, innovation, obs_weight, obs_count)
    ))


def body(background, obs_ens, innovation, obs_weight, obs_count, dest):
    return analyse(
        background, obs_ens, innovation, obs_weight, obs_count.T, dest.reshape(1, -1)
    )


def solution(mesh):
    return jax.shard_map(
        body,
        mesh=mesh,
        in_specs=(
            P("grp", "own", None),
            P("grp", "own", None),
            P("grp", "own"),
            P("grp", "own"),
            P("grp", "own"),
            P(),
        ),
        out_specs=P("grp", "own", None),
        check_vma=False,
    )
```

```python
import jax
import jax.numpy as jnp
from jax import lax
from jax.experimental import pallas as pl
from jax.experimental.pallas import tpu as pltpu
from jax.sharding import PartitionSpec as P

MESH = pl.DeviceIdType.MESH
F32 = jnp.float32
BF16 = jnp.bfloat16
MEMBERS = 512
B = 128
GROUPS_HERE = 8
ROUNDS = 2
GRP = 32
STRIDE = 12
OFF = [(0, 1), (0, 2), (0, 3), (1, 2), (1, 3), (2, 3)]
HALF = 4


def dot(a, b):
    return jnp.dot(a, b, preferred_element_type=F32)


def dot_nt(a, b):
    return lax.dot_general(a, b, (((1,), (1,)), ((), ())), preferred_element_type=F32)


def eye(n):
    rows = lax.broadcasted_iota(jnp.int32, (n, n), 0)
    cols = lax.broadcasted_iota(jnp.int32, (n, n), 1)
    return jnp.where(rows == cols, 1.0, 0.0).astype(F32)


def masks():
    rows = lax.broadcasted_iota(jnp.int32, (B, B), 0)
    cols = lax.broadcasted_iota(jnp.int32, (B, B), 1)
    return rows <= cols, rows == cols


def pack_diagonals(d):
    upper, middle = masks()
    pairs = [jnp.where(upper, d[i], d[i + 1]) for i in (0, 2)]
    lines = [jnp.sum(jnp.where(middle, d[i], 0.0), axis=0, keepdims=True) for i in (1, 3)]
    return pairs, lines


def unpack_diagonals(pairs, lines):
    upper, middle = masks()
    out = []
    for pair, line in zip(pairs, lines):
        turned = pair.T
        out.append(jnp.where(upper, pair, turned))
        out.append(jnp.where(middle, line, jnp.where(upper, turned, pair)))
    return out


def tile(row, lines):
    parts = [row[:, span(i)] for i in range(4)] + lines + [jnp.zeros((2, B), F32)]
    return jnp.concatenate(parts, axis=0)


def untile(small):
    row = jnp.concatenate([small[i : i + 1] for i in range(4)], axis=1)
    return row, [small[4:5], small[5:6]]


def span(i):
    return slice(i * B, (i + 1) * B)


def kernel(
    dest_hbm, obs_hbm, bg_hbm, innov_hbm, weight_hbm, count_hbm, out,
    dest, innov, obs_weight, count,
    obs, bg, wrow, src, part, own_part, relay_own, relay_in, owner_in, rhs_part, rhs_in,
    root, inv, fac, full, vbuf, mwbuf, pert, mean, spread, gathered, picked, holder_v, holder,
    obs_sem, bg_sem, send_z, recv_z, send_g, recv_g, self_sem, small_sem,
):
    me = lax.axis_index("grp")
    z = lax.axis_index("own")
    y, x, c = me // 8, lax.rem(me // 2, 4), lax.rem(me, 2)

    def peer(s):
        return (
            lax.rem(y + s // 8, 4) * 8
            + lax.rem(x + lax.rem(s // 2, 4), 4) * 2
            + lax.rem(c + lax.rem(s, 2), 2)
        )

    def step(i):
        return 1 + lax.rem(i * STRIDE, GRP - 1)

    def zpeer(q):
        return lax.rem(z + q, 4)

    def group(r, q):
        return zpeer(q) * ROUNDS + r

    barrier = pltpu.get_barrier_semaphore()

    def greet(s, carry):
        pl.semaphore_signal(barrier, inc=1, device_id={"grp": peer(s)}, device_id_type=MESH)
        return carry

    for q in (2, 1, 3):
        pl.semaphore_signal(barrier, inc=1, device_id={"own": zpeer(q)}, device_id_type=MESH)
    lax.fori_loop(1, GRP, greet, 0)

    small = (
        (count_hbm, count), (weight_hbm, obs_weight), (innov_hbm, innov), (dest_hbm, dest)
    )
    small = [
        pltpu.make_async_copy(pair[0], pair[1], small_sem.at[n]) for n, pair in enumerate(small)
    ]
    for load in small:
        load.start()
    loads = {}
    for r in range(ROUNDS):
        for q in (2, 1, 3, 0):
            loads[r, q] = pltpu.make_async_copy(
                obs_hbm.at[group(r, q)], obs.at[group(r, q)], obs_sem.at[r, q]
            )
            loads[r, q].start()
    bg_load = pltpu.make_async_copy(bg_hbm, bg, bg_sem)
    bg_load.start()

    for load in small:
        load.wait()
    position = lax.broadcasted_iota(jnp.int32, (1, 512), 1)
    for g in range(GROUPS_HERE):
        live = position < count[:, g : g + 1]
        weight = jnp.where(live, obs_weight[g : g + 1].astype(F32), 0.0)
        source = (weight * innov[g : g + 1].astype(F32)).astype(BF16).astype(F32)
        wrow[g] = jnp.broadcast_to(weight, (8, 512))
        src[g] = jnp.broadcast_to(source, (16, 512)).astype(BF16)

    pending = []

    def zcopy(source_ref, target_ref, q, r, index):
        copy = pltpu.make_async_remote_copy(
            src_ref=source_ref,
            dst_ref=target_ref,
            send_sem=send_z.at[r, index],
            recv_sem=recv_z.at[r, index],
            device_id={"own": zpeer(q)},
            device_id_type=MESH,
        )
        copy.start()
        pending.append(copy)
        return copy

    def gram(r, q):
        loads[r, q].wait()
        g = group(r, q)
        ens = obs[g].astype(F32)
        centred = (ens - jnp.mean(ens, axis=1, keepdims=True)).astype(BF16)
        turned = (centred.astype(F32).T * wrow[g][0:1]).astype(BF16)
        diagonal = []
        blocks = {}
        for i in range(4):
            strip = dot(turned[span(i)], centred[:, i * B :])
            diagonal.append(strip[:, :B])
            for j in range(i + 1, 4):
                blocks[i, j] = strip[:, (j - i) * B : (j - i + 1) * B]
        pairs, lines = pack_diagonals(diagonal)
        rhs_part[r, q] = tile(dot(src[g], centred)[0:1], lines)
        for b, block in enumerate([blocks[ij] for ij in OFF] + pairs):
            h, k = b // HALF, b % HALF
            if q == 0:
                own_part[r, b] = block
            elif (q, h) in ((1, 0), (3, 1)):
                relay_own[r, h, k] = block
            else:
                part[r, q, h, k] = block.astype(BF16)

    relay = {}
    direct = {}

    def send_parts(r, q):
        if q == 2:
            relay[r, 0] = zcopy(part.at[r, 2, 0], relay_in.at[r, 0], 1, r, 0)
            relay[r, 1] = zcopy(part.at[r, 2, 1], relay_in.at[r, 1], 3, r, 1)
        elif q == 1:
            direct[r, 1] = zcopy(part.at[r, 1, 1], owner_in.at[r, 0, 1], 1, r, 2)
        else:
            direct[r, 0] = zcopy(part.at[r, 3, 0], owner_in.at[r, 1, 0], 3, r, 3)
        direct[r, 1 + q] = zcopy(rhs_part.at[r, q], rhs_in.at[r, q], q, r, 3 + q)

    combined = {}

    def combine(r):
        for h, q in ((0, 1), (1, 3)):
            relay[r, h].wait_recv()
            part[r, q, h] = (relay_own[r, h] + relay_in[r, h].astype(F32)).astype(BF16)
            combined[r, h] = zcopy(
                part.at[r, q, h], owner_in.at[r, 0 if q == 1 else 1, h], q, r, 7 + h
            )

    gathers = {}
    forward = {}

    def newton(r):
        for h in range(2):
            direct[r, h].wait_recv()
            combined[r, h].wait_recv()
        for q in (1, 2, 3):
            direct[r, 1 + q].wait_recv()
        small = rhs_part[r, 0] + rhs_in[r, 1] + rhs_in[r, 2] + rhs_in[r, 3]
        right, lines = untile(small)
        squares = jnp.zeros((B, B), F32)
        for b in range(2 * HALF):
            h, k = b // HALF, b % HALF
            total = own_part[r, b] + owner_in[r, 0, h, k].astype(F32)
            total = total + owner_in[r, 1, h, k].astype(F32)
            own_part[r, b] = total
            if b < len(OFF):
                squares = squares + 2.0 * (total * total)
        diagonal = unpack_diagonals([own_part[r, 6], own_part[r, 7]], lines)
        diagonal = [d + (MEMBERS - 1.0) * eye(B) for d in diagonal]
        for d in diagonal:
            squares = squares + d * d
        scale = jnp.sqrt(jnp.full((1, 1), jnp.sum(squares), F32))
        per = 1.0 / scale
        for i in range(4):
            root[span(i), span(i)] = (diagonal[i] * per).astype(BF16)
        for b, (i, j) in enumerate(OFF):
            block = own_part[r, b] * per
            root[span(i), span(j)] = block.astype(BF16)
            root[span(j), span(i)] = block.T.astype(BF16)
        fac[...] = (1.5 * eye(MEMBERS) - 0.5 * root[...].astype(F32)).astype(BF16)
        inv[...] = fac[...]
        root[...] = dot(root[...], fac[...]).astype(BF16)
        for _ in range(2):
            fac[...] = (1.5 * eye(MEMBERS) - 0.5 * dot(inv[...], root[...])).astype(BF16)
            root[...] = dot(root[...], fac[...]).astype(BF16)
            inv[...] = dot(fac[...], inv[...]).astype(BF16)
        fac[...] = (1.5 * eye(MEMBERS) - 0.5 * dot(inv[...], root[...])).astype(BF16)
        inv[...] = dot(fac[...], inv[...]).astype(BF16)

        def through(rows):
            high = rows.astype(BF16)
            low = (rows - high.astype(F32)).astype(BF16)
            both = dot_nt(jnp.concatenate([high, low], axis=0), inv[...])
            return both[0:16] + both[16:32]

        weight_row = (through(through(jnp.broadcast_to(right, (16, MEMBERS)))) * per)[0:1]
        gain = jnp.sqrt((MEMBERS - 1.0) * per)

        def scaled(i, j):
            return inv[span(i), span(j)].astype(F32) * gain

        pairs, lines = pack_diagonals([scaled(i, i) for i in range(4)])
        mwbuf[r, 0] = tile(weight_row, lines)
        for b, block in enumerate([scaled(i, j) for i, j in OFF] + pairs):
            vbuf[r, 0, b // HALF, b % HALF] = block.astype(BF16)

    def gather(r):
        gathers[r, 3] = zcopy(vbuf.at[r, 0], vbuf.at[r, 3], 1, r, 9)
        gathers[r, 1] = zcopy(vbuf.at[r, 0], vbuf.at[r, 1], 3, r, 10)
        for q in (1, 2, 3):
            gathers[r, 3 + q] = zcopy(mwbuf.at[r, 0], mwbuf.at[r, 4 - q], q, r, 10 + q)

    def pass_on(r):
        gathers[r, 3].wait_recv()
        forward[r, 0] = zcopy(vbuf.at[r, 3, 0], vbuf.at[r, 2, 0], 1, r, 14)
        gathers[r, 1].wait_recv()
        forward[r, 1] = zcopy(vbuf.at[r, 1, 1], vbuf.at[r, 2, 1], 3, r, 15)
        for q in (1, 2, 3):
            gathers[r, 3 + q].wait_recv()

    def perturb():
        bg_load.wait()

        def one(g, carry):
            state = bg[g].astype(F32)
            centre = jnp.mean(state, axis=1, keepdims=True)
            pert[g] = (state - centre).astype(BF16)
            mean[g] = jnp.broadcast_to(centre, (256, B))
            return carry

        lax.fori_loop(0, GROUPS_HERE, one, 0)

    def index():
        total = GROUPS_HERE * GRP
        across = jnp.broadcast_to(dest[...], (total, total))
        down = across.T
        rows = lax.broadcasted_iota(jnp.int32, (total, total), 0)
        cols = lax.broadcasted_iota(jnp.int32, (total, total), 1)
        match = jnp.where((across == down) & (cols < rows), 1, 0)
        slot = down * GROUPS_HERE + jnp.sum(match, axis=1, keepdims=True)
        local = lax.rem(rows, GROUPS_HERE)
        owner = lax.rem(local // ROUNDS + 4 - z, 4)
        place = (lax.rem(local, ROUNDS) * 4 + owner) * GRP + rows // GROUPS_HERE
        chosen = jnp.where(slot == cols, place, 0)
        holder_v[...] = jnp.broadcast_to(jnp.sum(chosen, axis=0, keepdims=True), (8, total))
        copy = pltpu.make_async_copy(holder_v, holder, small_sem.at[4])
        copy.start()
        copy.wait()

    def gcopy(phase, s, source_ref, target_ref):
        return pltpu.make_async_remote_copy(
            src_ref=source_ref,
            dst_ref=target_ref,
            send_sem=send_g.at[phase, s],
            recv_sem=recv_g.at[phase, s],
            device_id={"grp": peer(s)},
            device_id_type=MESH,
        )

    def spread_copy(e, s):
        return gcopy(e, s, spread.at[e, peer(s)], gathered.at[e * GRP + me])

    def apply(r, q):
        g = group(r, q)
        e = r * 4 + q
        weight_row, lines = untile(mwbuf[r, q])
        pairs = [vbuf[r, q, 1, 2].astype(F32), vbuf[r, q, 1, 3].astype(F32)]
        for i, d in enumerate(unpack_diagonals(pairs, lines)):
            full[span(i), span(i)] = d.astype(BF16)
        for b, (i, j) in enumerate(OFF):
            block = vbuf[r, q, b // HALF, b % HALF]
            full[span(i), span(j)] = block
            full[span(j), span(i)] = block.T
        shift = jnp.sum(pert[g].astype(F32) * weight_row, axis=1, keepdims=True)
        shift = shift + mean[g][:, 0:1]
        for h in range(2):
            block = (dot(pert[g], full[:, h * 256 : (h + 1) * 256]) + shift).astype(BF16)
            for k in range(16):
                spread[e, h * 16 + k] = block[k * 16 : (k + 1) * 16]

        def launch(i, carry):
            spread_copy(e, step(i)).start()
            return carry

        lax.fori_loop(0, GRP - 1, launch, 0)
        mine = pltpu.make_async_copy(
            spread.at[e, me], gathered.at[e * GRP + me], self_sem.at[e]
        )
        mine.start()
        locals_.append(mine)

    locals_ = []
    for q in (2, 1, 3):
        gram(0, q)
        if q == 2:
            pl.semaphore_wait(barrier, GRP - 1 + 3)
        send_parts(0, q)
    gram(0, 0)
    for q in (2, 1, 3, 0):
        gram(1, q)
    combine(0)
    for q in (2, 1, 3):
        send_parts(1, q)
    perturb()
    index()
    newton(0)
    combine(1)
    gather(0)
    apply(0, 0)
    newton(1)
    gather(1)
    apply(1, 0)
    pass_on(0)
    apply(0, 1)
    apply(0, 3)
    pass_on(1)
    apply(1, 1)
    apply(1, 3)
    for r in range(ROUNDS):
        forward[r, 0].wait_recv()
        forward[r, 1].wait_recv()
        apply(r, 2)

    def landed(e, carry):
        def one(s, inner):
            spread_copy(e, s).wait_recv()
            return inner

        return lax.fori_loop(1, GRP, one, carry)

    lax.fori_loop(0, GROUPS_HERE, landed, 0)
    for copy in locals_:
        copy.wait()

    row = pl.multiple_of(lax.rem(me, 16) * 16, 16)
    col = pl.multiple_of((me // 16) * 256, 256)
    target = out.at[:, pl.ds(row, 16), pl.ds(col, 256)]

    def pick(d):
        for k in range(GROUPS_HERE):
            at = lax.clamp(0, holder[0, d * GROUPS_HERE + k], GROUPS_HERE * GRP - 1)
            picked[d, k] = gathered[at]

    def route(s):
        return gcopy(GROUPS_HERE, s, picked.at[peer(s)], target)

    pick(peer(step(0)))

    def move(i, carry):
        pick(peer(step(i + 1)))
        route(step(i)).start()
        return carry

    lax.fori_loop(0, GRP - 2, move, 0)
    pick(me)
    route(step(GRP - 2)).start()
    last = pltpu.make_async_copy(picked.at[me], target, self_sem.at[GROUPS_HERE])
    last.start()
    for copy in pending:
        copy.wait_send()

    def sent(e, carry):
        def one(s, inner):
            spread_copy(e, s).wait_send()
            return inner

        return lax.fori_loop(1, GRP, one, carry)

    lax.fori_loop(0, GROUPS_HERE, sent, 0)

    def done(s, carry):
        route(s).wait()
        return carry

    lax.fori_loop(1, GRP, done, 0)
    last.wait()


def analyse(background, obs_ens, innovation, obs_weight, obs_count, dest):
    vmem = pltpu.VMEM
    hbm_spec = pl.BlockSpec(memory_space=pltpu.HBM)
    return pl.pallas_call(
        kernel,
        out_shape=jax.ShapeDtypeStruct(background.shape, BF16),
        in_specs=[hbm_spec] * 6,
        out_specs=pl.BlockSpec(memory_space=pl.ANY),
        scratch_shapes=[
            vmem(dest.shape, jnp.int32),
            vmem(innovation.shape, BF16),
            vmem(obs_weight.shape, BF16),
            vmem(obs_count.shape, jnp.int32),
            vmem((8, 512, 512), BF16),
            vmem((8, 256, 512), BF16),
            vmem((8, 8, 512), F32),
            vmem((8, 16, 512), BF16),
            vmem((2, 4, 2, HALF, B, B), BF16),
            vmem((2, 2 * HALF, B, B), F32),
            vmem((2, 2, HALF, B, B), F32),
            vmem((2, 2, HALF, B, B), BF16),
            vmem((2, 2, 2, HALF, B, B), BF16),
            vmem((2, 4, 8, B), F32),
            vmem((2, 4, 8, B), F32),
            vmem((512, 512), BF16),
            vmem((512, 512), BF16),
            vmem((512, 512), BF16),
            vmem((512, 512), BF16),
            vmem((2, 4, 2, HALF, B, B), BF16),
            vmem((2, 4, 8, B), F32),
            vmem((8, 256, 512), BF16),
            vmem((8, 256, B), F32),
            vmem((8, 32, 16, 256), BF16),
            vmem((256, 16, 256), BF16),
            vmem((32, 8, 16, 256), BF16),
            vmem((8, 256), jnp.int32),
            pltpu.SMEM((8, 256), jnp.int32),
            pltpu.SemaphoreType.DMA((2, 4)),
            pltpu.SemaphoreType.DMA,
            pltpu.SemaphoreType.DMA((2, 16)),
            pltpu.SemaphoreType.DMA((2, 16)),
            pltpu.SemaphoreType.DMA((9, 32)),
            pltpu.SemaphoreType.DMA((9, 32)),
            pltpu.SemaphoreType.DMA((9,)),
            pltpu.SemaphoreType.DMA((5,)),
        ],
        compiler_params=pltpu.CompilerParams(
            collective_id=0, has_side_effects=True, vmem_limit_bytes=44 * 1024 * 1024
        ),
    )(*(
        pltpu.with_memory_space_constraint(a, pltpu.HBM)
        for a in (dest, obs_ens, background, innovation, obs_weight, obs_count)
    ))


def body(background, obs_ens, innovation, obs_weight, obs_count, dest):
    return analyse(
        background, obs_ens, innovation, obs_weight, obs_count.T, dest.reshape(1, -1)
    )


def solution(mesh):
    return jax.shard_map(
        body,
        mesh=mesh,
        in_specs=(
            P("grp", "own", None),
            P("grp", "own", None),
            P("grp", "own"),
            P("grp", "own"),
            P("grp", "own"),
            P(),
        ),
        out_specs=P("grp", "own", None),
        check_vma=False,
    )
```

```python
import jax
import jax.numpy as jnp
from jax import lax
from jax.experimental import pallas as pl
from jax.experimental.pallas import tpu as pltpu
from jax.sharding import PartitionSpec as P

MESH = pl.DeviceIdType.MESH
F32 = jnp.float32
BF16 = jnp.bfloat16
MEMBERS = 512
B = 128
GROUPS_HERE = 8
ROUNDS = 2
GRP = 32
STRIDE = 5
CORE, SIDE_X, SIDE_Y = (1,), (2, 6), (8, 24)
OFF = [(0, 1), (0, 2), (0, 3), (1, 2), (1, 3), (2, 3)]
HALF = 4


def dot(a, b):
    return jnp.dot(a, b, preferred_element_type=F32)


def dot_nt(a, b):
    return lax.dot_general(a, b, (((1,), (1,)), ((), ())), preferred_element_type=F32)


def eye(n):
    rows = lax.broadcasted_iota(jnp.int32, (n, n), 0)
    cols = lax.broadcasted_iota(jnp.int32, (n, n), 1)
    return jnp.where(rows == cols, 1.0, 0.0).astype(F32)


def masks():
    rows = lax.broadcasted_iota(jnp.int32, (B, B), 0)
    cols = lax.broadcasted_iota(jnp.int32, (B, B), 1)
    return rows <= cols, rows == cols


def pack_diagonals(d):
    upper, middle = masks()
    pairs = [jnp.where(upper, d[i], d[i + 1]) for i in (0, 2)]
    lines = [jnp.sum(jnp.where(middle, d[i], 0.0), axis=0, keepdims=True) for i in (1, 3)]
    return pairs, lines


def unpack_diagonals(pairs, lines):
    upper, middle = masks()
    out = []
    for pair, line in zip(pairs, lines):
        turned = pair.T
        out.append(jnp.where(upper, pair, turned))
        out.append(jnp.where(middle, line, jnp.where(upper, turned, pair)))
    return out


def tile(row, lines):
    parts = [row[:, span(i)] for i in range(4)] + lines + [jnp.zeros((2, B), F32)]
    return jnp.concatenate(parts, axis=0)


def untile(small):
    row = jnp.concatenate([small[i : i + 1] for i in range(4)], axis=1)
    return row, [small[4:5], small[5:6]]


def span(i):
    return slice(i * B, (i + 1) * B)


def kernel(
    dest_hbm, obs_hbm, bg_hbm, innov_hbm, weight_hbm, count_hbm, out,
    dest, innov, obs_weight, count,
    obs, bg, wrow, src, part, own_part, relay_own, relay_in, owner_in, rhs_part, rhs_in,
    root, inv, fac, full, vbuf, mwbuf, pert, mean, spread, gathered, picked, holder_v, holder,
    obs_sem, bg_sem, send_z, recv_z, send_g, recv_g, self_sem, small_sem, known,
):
    me = lax.axis_index("grp")
    z = lax.axis_index("own")
    y, x, c = me // 8, lax.rem(me // 2, 4), lax.rem(me, 2)

    def peer(s):
        return (
            lax.rem(y + s // 8, 4) * 8
            + lax.rem(x + lax.rem(s // 2, 4), 4) * 2
            + lax.rem(c + lax.rem(s, 2), 2)
        )

    def step(i):
        return 1 + lax.rem(i * STRIDE, GRP - 1)

    def zpeer(q):
        return lax.rem(z + q, 4)

    def group(r, q):
        return zpeer(q) * ROUNDS + r

    loads = {
        (r, q): pltpu.make_async_copy(
            obs_hbm.at[group(r, q)], obs.at[group(r, q)], obs_sem.at[r, q]
        )
        for r in range(ROUNDS)
        for q in (2, 1, 3, 0)
    }
    small = (
        (count_hbm, count), (weight_hbm, obs_weight), (innov_hbm, innov), (dest_hbm, dest)
    )
    small = [
        pltpu.make_async_copy(pair[0], pair[1], small_sem.at[n]) for n, pair in enumerate(small)
    ]
    bg_load = pltpu.make_async_copy(bg_hbm, bg, bg_sem)
    barrier = pltpu.get_barrier_semaphore()

    def tell(semaphore, neighbours):
        for s in neighbours:
            pl.semaphore_signal(semaphore, inc=1, device_id={"grp": peer(s)}, device_id_type=MESH)

    for q in (2, 1, 3):
        pl.semaphore_signal(barrier, inc=1, device_id={"own": zpeer(q)}, device_id_type=MESH)
    for load in small:
        load.start()
    loads[0, 2].start()
    tell(barrier, CORE + SIDE_X + SIDE_Y)
    loads[0, 1].start()
    loads[0, 3].start()

    for load in small:
        load.wait()
    position = lax.broadcasted_iota(jnp.int32, (1, 512), 1)
    for g in range(GROUPS_HERE):
        live = position < count[:, g : g + 1]
        weight = jnp.where(live, obs_weight[g : g + 1].astype(F32), 0.0)
        source = (weight * innov[g : g + 1].astype(F32)).astype(BF16).astype(F32)
        wrow[g] = jnp.broadcast_to(weight, (8, 512))
        src[g] = jnp.broadcast_to(source, (16, 512)).astype(BF16)

    pending = []

    def zcopy(source_ref, target_ref, q, r, index):
        copy = pltpu.make_async_remote_copy(
            src_ref=source_ref,
            dst_ref=target_ref,
            send_sem=send_z.at[r, index],
            recv_sem=recv_z.at[r, index],
            device_id={"own": zpeer(q)},
            device_id_type=MESH,
        )
        copy.start()
        pending.append(copy)
        return copy

    def gram(r, q):
        loads[r, q].wait()
        g = group(r, q)
        ens = obs[g].astype(F32)
        centred = (ens - jnp.mean(ens, axis=1, keepdims=True)).astype(BF16)
        turned = (centred.astype(F32).T * wrow[g][0:1]).astype(BF16)
        diagonal = []
        blocks = {}
        for i in range(4):
            strip = dot(turned[span(i)], centred[:, i * B :])
            diagonal.append(strip[:, :B])
            for j in range(i + 1, 4):
                blocks[i, j] = strip[:, (j - i) * B : (j - i + 1) * B]
        pairs, lines = pack_diagonals(diagonal)
        rhs_part[r, q] = tile(dot(src[g], centred)[0:1], lines)
        for b, block in enumerate([blocks[ij] for ij in OFF] + pairs):
            h, k = b // HALF, b % HALF
            if q == 0:
                own_part[r, b] = block
            elif (q, h) in ((1, 0), (3, 1)):
                relay_own[r, h, k] = block
            else:
                part[r, q, h, k] = block.astype(BF16)

    relay = {}
    direct = {}

    def send_parts(r, q):
        direct[r, 1 + q] = zcopy(rhs_part.at[r, q], rhs_in.at[r, q], q, r, 3 + q)
        if q == 2:
            relay[r, 0] = zcopy(part.at[r, 2, 0], relay_in.at[r, 0], 1, r, 0)
            relay[r, 1] = zcopy(part.at[r, 2, 1], relay_in.at[r, 1], 3, r, 1)
        elif q == 1:
            direct[r, 1] = zcopy(part.at[r, 1, 1], owner_in.at[r, 0, 1], 1, r, 2)
        else:
            direct[r, 0] = zcopy(part.at[r, 3, 0], owner_in.at[r, 1, 0], 3, r, 3)

    combined = {}

    def combine(r):
        for h, q in ((0, 1), (1, 3)):
            relay[r, h].wait_recv()
            part[r, q, h] = (relay_own[r, h] + relay_in[r, h].astype(F32)).astype(BF16)
            combined[r, h] = zcopy(
                part.at[r, q, h], owner_in.at[r, 0 if q == 1 else 1, h], q, r, 7 + h
            )

    gathers = {}
    forward = {}

    def newton(r):
        for h in range(2):
            direct[r, h].wait_recv()
            combined[r, h].wait_recv()
        for q in (1, 2, 3):
            direct[r, 1 + q].wait_recv()
        small = rhs_part[r, 0] + rhs_in[r, 1] + rhs_in[r, 2] + rhs_in[r, 3]
        right, lines = untile(small)
        squares = jnp.zeros((B, B), F32)
        for b in range(2 * HALF):
            h, k = b // HALF, b % HALF
            total = own_part[r, b] + owner_in[r, 0, h, k].astype(F32)
            total = total + owner_in[r, 1, h, k].astype(F32)
            own_part[r, b] = total
            if b < len(OFF):
                squares = squares + 2.0 * (total * total)
        diagonal = unpack_diagonals([own_part[r, 6], own_part[r, 7]], lines)
        diagonal = [d + (MEMBERS - 1.0) * eye(B) for d in diagonal]
        for d in diagonal:
            squares = squares + d * d
        scale = jnp.sqrt(jnp.full((1, 1), jnp.sum(squares), F32))
        per = 1.0 / scale
        for i in range(4):
            root[span(i), span(i)] = (diagonal[i] * per).astype(BF16)
        for b, (i, j) in enumerate(OFF):
            block = own_part[r, b] * per
            root[span(i), span(j)] = block.astype(BF16)
            root[span(j), span(i)] = block.T.astype(BF16)
        fac[...] = (1.5 * eye(MEMBERS) - 0.5 * root[...].astype(F32)).astype(BF16)
        inv[...] = fac[...]
        root[...] = dot(root[...], fac[...]).astype(BF16)
        for _ in range(2):
            fac[...] = (1.5 * eye(MEMBERS) - 0.5 * dot(inv[...], root[...])).astype(BF16)
            root[...] = dot(root[...], fac[...]).astype(BF16)
            inv[...] = dot(fac[...], inv[...]).astype(BF16)
        fac[...] = (1.5 * eye(MEMBERS) - 0.5 * dot(inv[...], root[...])).astype(BF16)
        inv[...] = dot(fac[...], inv[...]).astype(BF16)

        def through(rows):
            high = rows.astype(BF16)
            low = (rows - high.astype(F32)).astype(BF16)
            both = dot_nt(jnp.concatenate([high, low], axis=0), inv[...])
            return both[0:16] + both[16:32]

        weight_row = (through(through(jnp.broadcast_to(right, (16, MEMBERS)))) * per)[0:1]
        gain = jnp.sqrt((MEMBERS - 1.0) * per)

        def scaled(i, j):
            return inv[span(i), span(j)].astype(F32) * gain

        pairs, lines = pack_diagonals([scaled(i, i) for i in range(4)])
        mwbuf[r, 0] = tile(weight_row, lines)
        for b, block in enumerate([scaled(i, j) for i, j in OFF] + pairs):
            vbuf[r, 0, b // HALF, b % HALF] = block.astype(BF16)

    def gather(r):
        for q in (2, 1, 3):
            gathers[r, 3 + q] = zcopy(mwbuf.at[r, 0], mwbuf.at[r, 4 - q], q, r, 10 + q)
        gathers[r, 3] = zcopy(vbuf.at[r, 0], vbuf.at[r, 3], 1, r, 9)
        gathers[r, 1] = zcopy(vbuf.at[r, 0], vbuf.at[r, 1], 3, r, 10)

    def pass_on(r):
        gathers[r, 3].wait_recv()
        forward[r, 0] = zcopy(vbuf.at[r, 3, 0], vbuf.at[r, 2, 0], 1, r, 14)
        gathers[r, 1].wait_recv()
        forward[r, 1] = zcopy(vbuf.at[r, 1, 1], vbuf.at[r, 2, 1], 3, r, 15)
        gathers[r, 4].wait_recv()
        gathers[r, 6].wait_recv()

    def perturb():
        bg_load.wait()

        def one(g, carry):
            state = bg[g].astype(F32)
            centre = jnp.mean(state, axis=1, keepdims=True)
            pert[g] = (state - centre).astype(BF16)
            mean[g] = jnp.broadcast_to(centre, (256, B))
            return carry

        lax.fori_loop(0, GROUPS_HERE, one, 0)

    def index():
        total = GROUPS_HERE * GRP
        across = jnp.broadcast_to(dest[...], (total, total))
        down = across.T
        rows = lax.broadcasted_iota(jnp.int32, (total, total), 0)
        cols = lax.broadcasted_iota(jnp.int32, (total, total), 1)
        match = jnp.where((across == down) & (cols < rows), 1, 0)
        slot = down * GROUPS_HERE + jnp.sum(match, axis=1, keepdims=True)
        local = lax.rem(rows, GROUPS_HERE)
        owner = lax.rem(local // ROUNDS + 4 - z, 4)
        place = (lax.rem(local, ROUNDS) * 4 + owner) * GRP + rows // GROUPS_HERE
        chosen = jnp.where(slot == cols, place, 0)
        holder_v[...] = jnp.broadcast_to(jnp.sum(chosen, axis=0, keepdims=True), (8, total))
        copy = pltpu.make_async_copy(holder_v, holder, small_sem.at[4])
        copy.start()
        copy.wait()

    def gcopy(phase, s, source_ref, target_ref):
        return pltpu.make_async_remote_copy(
            src_ref=source_ref,
            dst_ref=target_ref,
            send_sem=send_g.at[phase, s],
            recv_sem=recv_g.at[phase, s],
            device_id={"grp": peer(s)},
            device_id_type=MESH,
        )

    def spread_copy(e, s):
        return gcopy(e, s, spread.at[e, peer(s)], gathered.at[e * GRP + me])

    def apply(r, q):
        g = group(r, q)
        e = r * 4 + q
        weight_row, lines = untile(mwbuf[r, q])
        pairs = [vbuf[r, q, 1, 2].astype(F32), vbuf[r, q, 1, 3].astype(F32)]
        for i, d in enumerate(unpack_diagonals(pairs, lines)):
            full[span(i), span(i)] = d.astype(BF16)
        for b, (i, j) in enumerate(OFF):
            block = vbuf[r, q, b // HALF, b % HALF]
            full[span(i), span(j)] = block
            full[span(j), span(i)] = block.T
        shift = jnp.sum(pert[g].astype(F32) * weight_row, axis=1, keepdims=True)
        shift = shift + mean[g][:, 0:1]
        for h in range(2):
            block = (dot(pert[g], full[:, h * 256 : (h + 1) * 256]) + shift).astype(BF16)
            for k in range(16):
                spread[e, h * 16 + k] = block[k * 16 : (k + 1) * 16]

        def launch(i, carry):
            spread_copy(e, step(i)).start()
            return carry

        lax.fori_loop(0, GRP - 1, launch, 0)
        mine = pltpu.make_async_copy(
            spread.at[e, me], gathered.at[e * GRP + me], self_sem.at[e]
        )
        mine.start()
        locals_.append(mine)

    locals_ = []
    for q in (2, 1, 3):
        gram(0, q)
        if q == 2:
            pl.semaphore_wait(barrier, 8)
            tell(known.at[0], SIDE_X)
        send_parts(0, q)
        if q == 2:
            loads[0, 0].start()
            for p in (2, 1, 3, 0):
                loads[1, p].start()
            bg_load.start()
    pl.semaphore_wait(known.at[0], 2)
    tell(known.at[1], SIDE_Y)
    gram(0, 0)
    for q in (2, 1, 3, 0):
        gram(1, q)
    combine(0)
    for q in (2, 1, 3):
        send_parts(1, q)
    pl.semaphore_wait(known.at[1], 2)
    tell(known.at[2], SIDE_Y)
    perturb()
    index()
    pl.semaphore_wait(known.at[2], 2)
    tell(known.at[3], CORE)
    newton(0)
    combine(1)
    gather(0)
    pl.semaphore_wait(known.at[3], 1)
    apply(0, 0)
    newton(1)
    gather(1)
    apply(1, 0)
    pass_on(0)
    apply(0, 1)
    apply(0, 3)
    pass_on(1)
    apply(1, 1)
    apply(1, 3)
    for r in range(ROUNDS):
        gathers[r, 5].wait_recv()
        forward[r, 0].wait_recv()
        forward[r, 1].wait_recv()
        apply(r, 2)

    def landed(e, carry):
        def one(s, inner):
            spread_copy(e, s).wait_recv()
            return inner

        return lax.fori_loop(1, GRP, one, carry)

    lax.fori_loop(0, GROUPS_HERE, landed, 0)
    for copy in locals_:
        copy.wait()

    row = pl.multiple_of(lax.rem(me, 16) * 16, 16)
    col = pl.multiple_of((me // 16) * 256, 256)
    target = out.at[:, pl.ds(row, 16), pl.ds(col, 256)]

    def pick(d):
        for k in range(GROUPS_HERE):
            at = lax.clamp(0, holder[0, d * GROUPS_HERE + k], GROUPS_HERE * GRP - 1)
            picked[d, k] = gathered[at]

    def route(s):
        return gcopy(GROUPS_HERE, s, picked.at[peer(s)], target)

    pick(peer(step(0)))

    def move(i, carry):
        pick(peer(step(i + 1)))
        route(step(i)).start()
        return carry

    lax.fori_loop(0, GRP - 2, move, 0)
    pick(me)
    route(step(GRP - 2)).start()
    last = pltpu.make_async_copy(picked.at[me], target, self_sem.at[GROUPS_HERE])
    last.start()
    for copy in pending:
        copy.wait_send()

    def sent(e, carry):
        def one(s, inner):
            spread_copy(e, s).wait_send()
            return inner

        return lax.fori_loop(1, GRP, one, carry)

    lax.fori_loop(0, GROUPS_HERE, sent, 0)

    def done(s, carry):
        route(s).wait()
        return carry

    lax.fori_loop(1, GRP, done, 0)
    last.wait()


def analyse(background, obs_ens, innovation, obs_weight, obs_count, dest):
    vmem = pltpu.VMEM
    hbm_spec = pl.BlockSpec(memory_space=pltpu.HBM)
    return pl.pallas_call(
        kernel,
        out_shape=jax.ShapeDtypeStruct(background.shape, BF16),
        in_specs=[hbm_spec] * 6,
        out_specs=pl.BlockSpec(memory_space=pl.ANY),
        scratch_shapes=[
            vmem(dest.shape, jnp.int32),
            vmem(innovation.shape, BF16),
            vmem(obs_weight.shape, BF16),
            vmem(obs_count.shape, jnp.int32),
            vmem((8, 512, 512), BF16),
            vmem((8, 256, 512), BF16),
            vmem((8, 8, 512), F32),
            vmem((8, 16, 512), BF16),
            vmem((2, 4, 2, HALF, B, B), BF16),
            vmem((2, 2 * HALF, B, B), F32),
            vmem((2, 2, HALF, B, B), F32),
            vmem((2, 2, HALF, B, B), BF16),
            vmem((2, 2, 2, HALF, B, B), BF16),
            vmem((2, 4, 8, B), F32),
            vmem((2, 4, 8, B), F32),
            vmem((512, 512), BF16),
            vmem((512, 512), BF16),
            vmem((512, 512), BF16),
            vmem((512, 512), BF16),
            vmem((2, 4, 2, HALF, B, B), BF16),
            vmem((2, 4, 8, B), F32),
            vmem((8, 256, 512), BF16),
            vmem((8, 256, B), F32),
            vmem((8, 32, 16, 256), BF16),
            vmem((256, 16, 256), BF16),
            vmem((32, 8, 16, 256), BF16),
            vmem((8, 256), jnp.int32),
            pltpu.SMEM((8, 256), jnp.int32),
            pltpu.SemaphoreType.DMA((2, 4)),
            pltpu.SemaphoreType.DMA,
            pltpu.SemaphoreType.DMA((2, 16)),
            pltpu.SemaphoreType.DMA((2, 16)),
            pltpu.SemaphoreType.DMA((9, 32)),
            pltpu.SemaphoreType.DMA((9, 32)),
            pltpu.SemaphoreType.DMA((9,)),
            pltpu.SemaphoreType.DMA((5,)),
            pltpu.SemaphoreType.REGULAR((4,)),
        ],
        compiler_params=pltpu.CompilerParams(
            collective_id=0, has_side_effects=True, vmem_limit_bytes=44 * 1024 * 1024
        ),
    )(*(
        pltpu.with_memory_space_constraint(a, pltpu.HBM)
        for a in (dest, obs_ens, background, innovation, obs_weight, obs_count)
    ))


def body(background, obs_ens, innovation, obs_weight, obs_count, dest):
    return analyse(
        background, obs_ens, innovation, obs_weight, obs_count.T, dest.reshape(1, -1)
    )


def solution(mesh):
    return jax.shard_map(
        body,
        mesh=mesh,
        in_specs=(
            P("grp", "own", None),
            P("grp", "own", None),
            P("grp", "own"),
            P("grp", "own"),
            P("grp", "own"),
            P(),
        ),
        out_specs=P("grp", "own", None),
        check_vma=False,
    )
```

```python
import jax
import jax.numpy as jnp
from jax import lax
from jax.experimental import pallas as pl
from jax.experimental.pallas import tpu as pltpu
from jax.sharding import PartitionSpec as P

MESH = pl.DeviceIdType.MESH
F32 = jnp.float32
BF16 = jnp.bfloat16
MEMBERS = 512
B = 128
GROUPS_HERE = 8
ROUNDS = 2
GRP = 32
STRIDE = 5
CORE, SIDE_X, SIDE_Y = (1,), (2, 6), (8, 24)
OFF = [(0, 1), (0, 2), (0, 3), (1, 2), (1, 3), (2, 3)]
HALF = 4


def dot(a, b):
    return jnp.dot(a, b, preferred_element_type=F32)


def dot_nt(a, b):
    return lax.dot_general(a, b, (((1,), (1,)), ((), ())), preferred_element_type=F32)


def eye(n):
    rows = lax.broadcasted_iota(jnp.int32, (n, n), 0)
    cols = lax.broadcasted_iota(jnp.int32, (n, n), 1)
    return jnp.where(rows == cols, 1.0, 0.0).astype(F32)


def masks():
    rows = lax.broadcasted_iota(jnp.int32, (B, B), 0)
    cols = lax.broadcasted_iota(jnp.int32, (B, B), 1)
    return rows <= cols, rows == cols


def pack_diagonals(d):
    upper, middle = masks()
    pairs = [jnp.where(upper, d[i], d[i + 1]) for i in (0, 2)]
    lines = [jnp.sum(jnp.where(middle, d[i], 0.0), axis=0, keepdims=True) for i in (1, 3)]
    return pairs, lines


def unpack_diagonals(pairs, lines):
    upper, middle = masks()
    out = []
    for pair, line in zip(pairs, lines):
        turned = pair.T
        out.append(jnp.where(upper, pair, turned))
        out.append(jnp.where(middle, line, jnp.where(upper, turned, pair)))
    return out


def tile(row, lines):
    parts = [row[:, span(i)] for i in range(4)] + lines + [jnp.zeros((2, B), F32)]
    return jnp.concatenate(parts, axis=0)


def untile(small):
    row = jnp.concatenate([small[i : i + 1] for i in range(4)], axis=1)
    return row, [small[4:5], small[5:6]]


def span(i):
    return slice(i * B, (i + 1) * B)


def kernel(
    dest_hbm, obs_hbm, bg_hbm, innov_hbm, weight_hbm, count_hbm, out,
    dest, innov, obs_weight, count,
    obs, bg, wrow, src, part, own_part, relay_own, relay_in, owner_in, rhs_part, rhs_in,
    root, inv, fac, full, vbuf, mwbuf, pert, mean, spread, gathered, picked, holder_v, holder,
    obs_sem, bg_sem, send_z, recv_z, send_g, recv_g, self_sem, small_sem, known,
):
    me = lax.axis_index("grp")
    z = lax.axis_index("own")
    y, x, c = me // 8, lax.rem(me // 2, 4), lax.rem(me, 2)

    def peer(s):
        return (
            lax.rem(y + s // 8, 4) * 8
            + lax.rem(x + lax.rem(s // 2, 4), 4) * 2
            + lax.rem(c + lax.rem(s, 2), 2)
        )

    def step(i):
        return 1 + lax.rem(i * STRIDE, GRP - 1)

    def zpeer(q):
        return lax.rem(z + q, 4)

    def group(r, q):
        return zpeer(q) * ROUNDS + r

    loads = {
        (r, q): pltpu.make_async_copy(
            obs_hbm.at[group(r, q)], obs.at[group(r, q)], obs_sem.at[r, q]
        )
        for r in range(ROUNDS)
        for q in (2, 1, 3, 0)
    }
    small = (
        (count_hbm, count), (weight_hbm, obs_weight), (innov_hbm, innov), (dest_hbm, dest)
    )
    small = [
        pltpu.make_async_copy(pair[0], pair[1], small_sem.at[n]) for n, pair in enumerate(small)
    ]
    bg_load = pltpu.make_async_copy(bg_hbm, bg, bg_sem)
    barrier = pltpu.get_barrier_semaphore()

    def tell(semaphore, neighbours):
        for s in neighbours:
            pl.semaphore_signal(semaphore, inc=1, device_id={"grp": peer(s)}, device_id_type=MESH)

    for q in (2, 1, 3):
        pl.semaphore_signal(barrier, inc=1, device_id={"own": zpeer(q)}, device_id_type=MESH)
    for load in small:
        load.start()
    loads[0, 2].start()
    tell(barrier, CORE + SIDE_X + SIDE_Y)
    loads[0, 1].start()
    loads[0, 3].start()

    for load in small:
        load.wait()
    position = lax.broadcasted_iota(jnp.int32, (1, 512), 1)
    for g in range(GROUPS_HERE):
        live = position < count[:, g : g + 1]
        weight = jnp.where(live, obs_weight[g : g + 1].astype(F32), 0.0)
        source = (weight * innov[g : g + 1].astype(F32)).astype(BF16).astype(F32)
        wrow[g] = jnp.broadcast_to(weight, (8, 512))
        src[g] = jnp.broadcast_to(source, (16, 512)).astype(BF16)

    pending = []

    def zcopy(source_ref, target_ref, q, r, index):
        copy = pltpu.make_async_remote_copy(
            src_ref=source_ref,
            dst_ref=target_ref,
            send_sem=send_z.at[r, index],
            recv_sem=recv_z.at[r, index],
            device_id={"own": zpeer(q)},
            device_id_type=MESH,
        )
        copy.start()
        pending.append(copy)
        return copy

    def gram(r, q):
        loads[r, q].wait()
        g = group(r, q)
        ens = obs[g].astype(F32)
        centred = (ens - jnp.mean(ens, axis=1, keepdims=True)).astype(BF16)
        turned = (centred.astype(F32).T * wrow[g][0:1]).astype(BF16)
        diagonal = []
        blocks = {}
        for i in range(4):
            strip = dot(turned[span(i)], centred[:, i * B :])
            diagonal.append(strip[:, :B])
            for j in range(i + 1, 4):
                blocks[i, j] = strip[:, (j - i) * B : (j - i + 1) * B]
        pairs, lines = pack_diagonals(diagonal)
        rhs_part[r, q] = tile(dot(src[g], centred)[0:1], lines)
        for b, block in enumerate([blocks[ij] for ij in OFF] + pairs):
            h, k = b // HALF, b % HALF
            if q == 0:
                own_part[r, b] = block
            elif (q, h) in ((1, 0), (3, 1)):
                relay_own[r, h, k] = block
            else:
                part[r, q, h, k] = block.astype(BF16)

    relay = {}
    direct = {}

    def send_parts(r, q):
        direct[r, 1 + q] = zcopy(rhs_part.at[r, q], rhs_in.at[r, q], q, r, 3 + q)
        if q == 2:
            relay[r, 0] = zcopy(part.at[r, 2, 0], relay_in.at[r, 0], 1, r, 0)
            relay[r, 1] = zcopy(part.at[r, 2, 1], relay_in.at[r, 1], 3, r, 1)
        elif q == 1:
            direct[r, 1] = zcopy(part.at[r, 1, 1], owner_in.at[r, 0, 1], 1, r, 2)
        else:
            direct[r, 0] = zcopy(part.at[r, 3, 0], owner_in.at[r, 1, 0], 3, r, 3)

    combined = {}

    def combine(r):
        for h, q in ((0, 1), (1, 3)):
            relay[r, h].wait_recv()
            part[r, q, h] = (relay_own[r, h] + relay_in[r, h].astype(F32)).astype(BF16)
            combined[r, h] = zcopy(
                part.at[r, q, h], owner_in.at[r, 0 if q == 1 else 1, h], q, r, 7 + h
            )

    gathers = {}
    forward = {}

    def newton(r):
        for h in range(2):
            direct[r, h].wait_recv()
            combined[r, h].wait_recv()
        for q in (1, 2, 3):
            direct[r, 1 + q].wait_recv()
        small = rhs_part[r, 0] + rhs_in[r, 1] + rhs_in[r, 2] + rhs_in[r, 3]
        right, lines = untile(small)
        squares = jnp.zeros((B, B), F32)
        for b in range(2 * HALF):
            h, k = b // HALF, b % HALF
            total = own_part[r, b] + owner_in[r, 0, h, k].astype(F32)
            total = total + owner_in[r, 1, h, k].astype(F32)
            own_part[r, b] = total
            if b < len(OFF):
                squares = squares + 2.0 * (total * total)
        diagonal = unpack_diagonals([own_part[r, 6], own_part[r, 7]], lines)
        diagonal = [d + (MEMBERS - 1.0) * eye(B) for d in diagonal]
        for d in diagonal:
            squares = squares + d * d
        scale = jnp.sqrt(jnp.full((1, 1), jnp.sum(squares), F32))
        per = 1.0 / scale
        for i in range(4):
            root[span(i), span(i)] = (diagonal[i] * per).astype(BF16)
        for b, (i, j) in enumerate(OFF):
            block = own_part[r, b] * per
            root[span(i), span(j)] = block.astype(BF16)
            root[span(j), span(i)] = block.T.astype(BF16)
        fac[...] = (1.5 * eye(MEMBERS) - 0.5 * root[...].astype(F32)).astype(BF16)
        inv[...] = fac[...]
        root[...] = dot(root[...], fac[...]).astype(BF16)
        for _ in range(2):
            fac[...] = (1.5 * eye(MEMBERS) - 0.5 * dot(inv[...], root[...])).astype(BF16)
            root[...] = dot(root[...], fac[...]).astype(BF16)
            inv[...] = dot(fac[...], inv[...]).astype(BF16)
        fac[...] = (1.5 * eye(MEMBERS) - 0.5 * dot(inv[...], root[...])).astype(BF16)
        inv[...] = dot(fac[...], inv[...]).astype(BF16)

        def through(rows):
            high = rows.astype(BF16)
            low = (rows - high.astype(F32)).astype(BF16)
            both = dot_nt(jnp.concatenate([high, low], axis=0), inv[...])
            return both[0:16] + both[16:32]

        weight_row = (through(through(jnp.broadcast_to(right, (16, MEMBERS)))) * per)[0:1]
        gain = jnp.sqrt((MEMBERS - 1.0) * per)

        def scaled(i, j):
            return inv[span(i), span(j)].astype(F32) * gain

        pairs, lines = pack_diagonals([scaled(i, i) for i in range(4)])
        mwbuf[r, 0] = tile(weight_row, lines)
        for b, block in enumerate([scaled(i, j) for i, j in OFF] + pairs):
            vbuf[r, 0, b // HALF, b % HALF] = block.astype(BF16)

    def gather(r):
        for q in (2, 1, 3):
            gathers[r, 3 + q] = zcopy(mwbuf.at[r, 0], mwbuf.at[r, 4 - q], q, r, 10 + q)
        gathers[r, 3] = zcopy(vbuf.at[r, 0], vbuf.at[r, 3], 1, r, 9)
        gathers[r, 1] = zcopy(vbuf.at[r, 0], vbuf.at[r, 1], 3, r, 10)

    def pass_on(r):
        gathers[r, 3].wait_recv()
        forward[r, 0] = zcopy(vbuf.at[r, 3, 0], vbuf.at[r, 2, 0], 1, r, 14)
        gathers[r, 1].wait_recv()
        forward[r, 1] = zcopy(vbuf.at[r, 1, 1], vbuf.at[r, 2, 1], 3, r, 15)
        gathers[r, 4].wait_recv()
        gathers[r, 6].wait_recv()

    def perturb():
        bg_load.wait()

        def one(g, carry):
            state = bg[g].astype(F32)
            centre = jnp.mean(state, axis=1, keepdims=True)
            pert[g] = (state - centre).astype(BF16)
            mean[g] = jnp.broadcast_to(centre, (256, B))
            return carry

        lax.fori_loop(0, GROUPS_HERE, one, 0)

    def index():
        total = GROUPS_HERE * GRP
        across = jnp.broadcast_to(dest[...], (total, total))
        down = across.T
        rows = lax.broadcasted_iota(jnp.int32, (total, total), 0)
        cols = lax.broadcasted_iota(jnp.int32, (total, total), 1)
        match = jnp.where((across == down) & (cols < rows), 1, 0)
        slot = down * GROUPS_HERE + jnp.sum(match, axis=1, keepdims=True)
        local = lax.rem(rows, GROUPS_HERE)
        owner = lax.rem(local // ROUNDS + 4 - z, 4)
        place = (lax.rem(local, ROUNDS) * 4 + owner) * GRP + rows // GROUPS_HERE
        chosen = jnp.where(slot == cols, place, 0)
        holder_v[...] = jnp.broadcast_to(jnp.sum(chosen, axis=0, keepdims=True), (8, total))
        copy = pltpu.make_async_copy(holder_v, holder, small_sem.at[4])
        copy.start()
        copy.wait()

    def gcopy(phase, s, source_ref, target_ref):
        return pltpu.make_async_remote_copy(
            src_ref=source_ref,
            dst_ref=target_ref,
            send_sem=send_g.at[phase, s],
            recv_sem=recv_g.at[phase, s],
            device_id={"grp": peer(s)},
            device_id_type=MESH,
        )

    def spread_copy(e, s):
        return gcopy(e, s, spread.at[e, peer(s)], gathered.at[e * GRP + me])

    def apply(r, q):
        g = group(r, q)
        e = r * 4 + q
        weight_row, lines = untile(mwbuf[r, q])
        pairs = [vbuf[r, q, 1, 2].astype(F32), vbuf[r, q, 1, 3].astype(F32)]
        for i, d in enumerate(unpack_diagonals(pairs, lines)):
            full[span(i), span(i)] = d.astype(BF16)
        for b, (i, j) in enumerate(OFF):
            block = vbuf[r, q, b // HALF, b % HALF]
            full[span(i), span(j)] = block
            full[span(j), span(i)] = block.T
        shift = jnp.sum(pert[g].astype(F32) * weight_row, axis=1, keepdims=True)
        shift = shift + mean[g][:, 0:1]
        for h in range(2):
            block = (dot(pert[g], full[:, h * 256 : (h + 1) * 256]) + shift).astype(BF16)
            for k in range(16):
                spread[e, h * 16 + k] = block[k * 16 : (k + 1) * 16]

        def launch(i, carry):
            spread_copy(e, step(i + 7 * e)).start()
            return carry

        lax.fori_loop(0, GRP - 1, launch, 0)
        mine = pltpu.make_async_copy(
            spread.at[e, me], gathered.at[e * GRP + me], self_sem.at[e]
        )
        mine.start()
        locals_.append(mine)

    locals_ = []
    for q in (2, 1, 3):
        gram(0, q)
        if q == 2:
            pl.semaphore_wait(barrier, 8)
            tell(known.at[0], SIDE_X)
        send_parts(0, q)
        if q == 2:
            loads[0, 0].start()
            for p in (2, 1, 3, 0):
                loads[1, p].start()
            bg_load.start()
    pl.semaphore_wait(known.at[0], 2)
    tell(known.at[1], SIDE_Y)
    gram(0, 0)
    for q in (2, 1, 3, 0):
        gram(1, q)
    combine(0)
    for q in (2, 1, 3):
        send_parts(1, q)
    pl.semaphore_wait(known.at[1], 2)
    tell(known.at[2], SIDE_Y)
    perturb()
    index()
    pl.semaphore_wait(known.at[2], 2)
    tell(known.at[3], CORE)
    newton(0)
    combine(1)
    gather(0)
    pl.semaphore_wait(known.at[3], 1)
    apply(0, 0)
    newton(1)
    gather(1)
    apply(1, 0)
    pass_on(0)
    apply(0, 1)
    apply(0, 3)
    pass_on(1)
    apply(1, 1)
    apply(1, 3)
    for r in range(ROUNDS):
        gathers[r, 5].wait_recv()
        forward[r, 0].wait_recv()
        forward[r, 1].wait_recv()
        apply(r, 2)

    def landed(e, carry):
        def one(s, inner):
            spread_copy(e, s).wait_recv()
            return inner

        return lax.fori_loop(1, GRP, one, carry)

    lax.fori_loop(0, GROUPS_HERE, landed, 0)
    for copy in locals_:
        copy.wait()

    row = pl.multiple_of(lax.rem(me, 16) * 16, 16)
    col = pl.multiple_of((me // 16) * 256, 256)
    target = out.at[:, pl.ds(row, 16), pl.ds(col, 256)]

    def pick(d):
        for k in range(GROUPS_HERE):
            at = lax.clamp(0, holder[0, d * GROUPS_HERE + k], GROUPS_HERE * GRP - 1)
            picked[d, k] = gathered[at]

    def route(s):
        return gcopy(GROUPS_HERE, s, picked.at[peer(s)], target)

    pick(peer(step(0)))

    def move(i, carry):
        pick(peer(step(i + 1)))
        route(step(i)).start()
        return carry

    lax.fori_loop(0, GRP - 2, move, 0)
    pick(me)
    route(step(GRP - 2)).start()
    last = pltpu.make_async_copy(picked.at[me], target, self_sem.at[GROUPS_HERE])
    last.start()
    for copy in pending:
        copy.wait_send()

    def sent(e, carry):
        def one(s, inner):
            spread_copy(e, s).wait_send()
            return inner

        return lax.fori_loop(1, GRP, one, carry)

    lax.fori_loop(0, GROUPS_HERE, sent, 0)

    def done(s, carry):
        route(s).wait()
        return carry

    lax.fori_loop(1, GRP, done, 0)
    last.wait()


def analyse(background, obs_ens, innovation, obs_weight, obs_count, dest):
    vmem = pltpu.VMEM
    hbm_spec = pl.BlockSpec(memory_space=pltpu.HBM)
    return pl.pallas_call(
        kernel,
        out_shape=jax.ShapeDtypeStruct(background.shape, BF16),
        in_specs=[hbm_spec] * 6,
        out_specs=pl.BlockSpec(memory_space=pl.ANY),
        scratch_shapes=[
            vmem(dest.shape, jnp.int32),
            vmem(innovation.shape, BF16),
            vmem(obs_weight.shape, BF16),
            vmem(obs_count.shape, jnp.int32),
            vmem((8, 512, 512), BF16),
            vmem((8, 256, 512), BF16),
            vmem((8, 8, 512), F32),
            vmem((8, 16, 512), BF16),
            vmem((2, 4, 2, HALF, B, B), BF16),
            vmem((2, 2 * HALF, B, B), F32),
            vmem((2, 2, HALF, B, B), F32),
            vmem((2, 2, HALF, B, B), BF16),
            vmem((2, 2, 2, HALF, B, B), BF16),
            vmem((2, 4, 8, B), F32),
            vmem((2, 4, 8, B), F32),
            vmem((512, 512), BF16),
            vmem((512, 512), BF16),
            vmem((512, 512), BF16),
            vmem((512, 512), BF16),
            vmem((2, 4, 2, HALF, B, B), BF16),
            vmem((2, 4, 8, B), F32),
            vmem((8, 256, 512), BF16),
            vmem((8, 256, B), F32),
            vmem((8, 32, 16, 256), BF16),
            vmem((256, 16, 256), BF16),
            vmem((32, 8, 16, 256), BF16),
            vmem((8, 256), jnp.int32),
            pltpu.SMEM((8, 256), jnp.int32),
            pltpu.SemaphoreType.DMA((2, 4)),
            pltpu.SemaphoreType.DMA,
            pltpu.SemaphoreType.DMA((2, 16)),
            pltpu.SemaphoreType.DMA((2, 16)),
            pltpu.SemaphoreType.DMA((9, 32)),
            pltpu.SemaphoreType.DMA((9, 32)),
            pltpu.SemaphoreType.DMA((9,)),
            pltpu.SemaphoreType.DMA((5,)),
            pltpu.SemaphoreType.REGULAR((4,)),
        ],
        compiler_params=pltpu.CompilerParams(
            collective_id=0, has_side_effects=True, vmem_limit_bytes=44 * 1024 * 1024
        ),
    )(*(
        pltpu.with_memory_space_constraint(a, pltpu.HBM)
        for a in (dest, obs_ens, background, innovation, obs_weight, obs_count)
    ))


def body(background, obs_ens, innovation, obs_weight, obs_count, dest):
    return analyse(
        background, obs_ens, innovation, obs_weight, obs_count.T, dest.reshape(1, -1)
    )


def solution(mesh):
    return jax.shard_map(
        body,
        mesh=mesh,
        in_specs=(
            P("grp", "own", None),
            P("grp", "own", None),
            P("grp", "own"),
            P("grp", "own"),
            P("grp", "own"),
            P(),
        ),
        out_specs=P("grp", "own", None),
        check_vma=False,
    )
```
